512 devices in a mesh: seq: 128 (over x_hi, z, y), head: 4 (over x_lo, core).
Axes of the slice: x: 4 (x_hi: 2, x_lo: 2; x = x_hi * 2 + x_lo), y: 4, z: 16, core: 2. Of those that a mesh axis runs over, the one named last changes fastest.
Arguments:
- layer_input: bfloat16 [16384, 2688], P('seq'), may hold values from -32 to 32
- grad_out: bfloat16 [16384, 2688], P('seq'), may hold values from -6 to 6
- doc_start: int32 [16384], P('seq'), may hold values from 0 to 16383, as said below
- w_query: bfloat16 [2688, 2048], P('seq', 'head'), may hold values from -0.125 to 0.125
- key_weight: bfloat16 [2688, 1024], P('seq', 'head'), may hold values from -0.125 to 0.125
- value_weight: bfloat16 [2688, 1024], P('seq', 'head'), may hold values from -0.125 to 0.125
- w_out: bfloat16 [2048, 2688], P('head', 'seq'), may hold values from -0.125 to 0.125
- q_gain: float32 [128], replicated, may hold values from 0.5 to 5, as said below
- key_norm_gain: float32 [128], replicated, may hold values from 0.5 to 5, as said below
Outputs:
- fisher_value: float32 [2688, 1024], P('seq', 'head')
- grad_input: bfloat16 [16384, 2688], P(('seq', 'head'))
The draws below stay inside these ranges and needn't reach their ends.
Inputs may be any that keep to these rules, and one draw needn't show every extreme that they name: doc_start[t] is the first token of the document holding token t: it never falls, doc_start[t] <= t, doc_start[0] = 0, and the last token begins a document of its own. `q_gain`: positive. `key_norm_gain`: positive.
All inputs are finite; a program needn't handle non-finite values.
Results may differ from the reference program's by a relative error of at most 0.011.
Values may be sent and summed in bfloat16 or wider, within the bound.
A program may use at most 64 MiB of HBM per device.

```python
import math
import jax
import jax.numpy as jnp
from jax import lax

MODEL_WIDTH = 2688
QUERY_HEADS = 16
KEY_VALUE_HEADS = 8
HEAD_SIZE = 128
QSCALE = 168
WINDOW = 1024
TOK_DEV = 128
REACH = 8
TOKENS = 16384


def draw_doc_start(key, part):
    begins = jax.random.randint(jax.random.fold_in(key, 3), (TOKENS,), 0, WINDOW) == 0
    begins = begins.at[0].set(True)
    begins = begins.at[TOKENS - 1].set(True)
    marks = jnp.where(begins, jnp.arange(TOKENS, dtype=jnp.int32), 0)
    return lax.cummax(marks, axis=0).astype(jnp.int32)


def position_scale(key):
    starts = draw_doc_start(key, 0)
    offset = (jnp.arange(TOKENS, dtype=jnp.int32) - starts).astype(jnp.float32)
    slow_part = jnp.exp(0.5 - 1.2 * jnp.minimum(1.0, offset / float(WINDOW)))
    early_part = 1.0 + 1.5 * jnp.exp(-offset * (16.0 / float(WINDOW)))
    return slow_part * early_part


def draw_layer_input(key, part):
    blocks = TOKENS // TOK_DEV
    noise = jnp.clip(jax.random.normal(jax.random.fold_in(key, 21), (TOKENS, MODEL_WIDTH), jnp.float32), -4.0, 4.0)
    pairing = jax.random.permutation(jax.random.fold_in(key, 23), blocks)
    row_block = jnp.arange(TOKENS, dtype=jnp.int32) // TOK_DEV
    col_block = jnp.arange(MODEL_WIDTH, dtype=jnp.int32) // (MODEL_WIDTH // blocks)
    spike = jnp.where(col_block[None, :] == pairing[row_block][:, None], 2.5, 1.0)
    values = noise * spike * position_scale(key)[:, None]
    return jnp.clip(values, -32.0, 32.0).astype(jnp.bfloat16)


def draw_q_gain(key, part):
    gains = jnp.exp(jax.random.uniform(jax.random.fold_in(key, 1), (HEAD_SIZE,), jnp.float32, -0.4, 0.4))
    return gains.astype(jnp.float32)


def draw_key_norm_gain(key, part):
    gains = jnp.exp(jax.random.uniform(jax.random.fold_in(key, 2), (HEAD_SIZE,), jnp.float32, -0.4, 0.4))
    return gains.astype(jnp.float32)


def block_levels(own_key, shape, cuts, least, high):
    level = 1.0
    for axis_at, parts in cuts:
        draws = jax.random.uniform(jax.random.fold_in(jax.random.fold_in(own_key, 6), axis_at), (parts,), jnp.float32, least / len(cuts), high / len(cuts))
        level = level * jnp.repeat(jnp.exp(draws), shape[axis_at] // parts).reshape((-1,) + (1,) * (len(shape) - 1 - axis_at))
    return level


def normal_values(stream_key, dims, scale, reach, shards=(), kind=jnp.bfloat16):
    loudness = block_levels(stream_key, dims, shards, -0.22, 0.18) if shards else 1.0
    values = jax.random.normal(stream_key, dims, jnp.float32) * scale * loudness
    return jnp.minimum(jnp.maximum(values, -reach), reach).astype(kind)


def setup_inputs(seed: int = 0) -> dict:
    key_of = jax.random.split(jax.random.key(seed), 10)
    return {
        "layer_input": draw_layer_input(jax.random.fold_in(key_of[9], 71), 0),
        "grad_out": normal_values(key_of[1], (TOKENS, MODEL_WIDTH), 1.0, 6.0, ((0, 128),)),
        "doc_start": draw_doc_start(jax.random.fold_in(key_of[9], 71), 0),
        "w_query": normal_values(key_of[3], (MODEL_WIDTH, QUERY_HEADS * HEAD_SIZE), MODEL_WIDTH ** -0.5, 0.125, ((0, 128), (1, 4))),
        "key_weight": normal_values(key_of[4], (MODEL_WIDTH, KEY_VALUE_HEADS * HEAD_SIZE), MODEL_WIDTH ** -0.5, 0.125, ((0, 128), (1, 4))),
        "value_weight": normal_values(key_of[5], (MODEL_WIDTH, KEY_VALUE_HEADS * HEAD_SIZE), MODEL_WIDTH ** -0.5, 0.125, ((0, 128), (1, 4))),
        "w_out": normal_values(key_of[6], (QUERY_HEADS * HEAD_SIZE, MODEL_WIDTH), (QUERY_HEADS * HEAD_SIZE) ** -0.5, 0.125, ((0, 4), (1, 128))),
        "q_gain": draw_q_gain(jax.random.fold_in(key_of[9], 71), 0),
        "key_norm_gain": draw_key_norm_gain(jax.random.fold_in(key_of[9], 71), 0),
    }


def rotary_normed(unrotated_rows, gain_vec, token_positions, head_count):
    tokens_here = unrotated_rows.shape[0]
    entries = unrotated_rows.reshape(tokens_here, head_count, HEAD_SIZE)
    mean_sq = lax.optimization_barrier(jnp.mean(entries * entries, axis=-1, keepdims=True))
    normed = entries * lax.rsqrt(mean_sq + 1e-06) * gain_vec
    half_dim = HEAD_SIZE // 2
    frequency = jnp.exp(jnp.arange(half_dim).astype(jnp.float32) * (-math.log(10000.0) / half_dim))
    angles = token_positions.astype(jnp.float32)[:, None] * frequency[None, :]
    cosine = jnp.cos(angles)[:, None, :]
    sine_part = jnp.sin(angles)[:, None, :]
    first_half = normed[..., :half_dim]
    second_half = normed[..., half_dim:]
    return jnp.concatenate([first_half * cosine - second_half * sine_part, second_half * cosine + first_half * sine_part], axis=-1)

def attend(query_blk, key_blk, value_blk, dattn_blk, visible):
    scale = float(QSCALE) ** (-0.5)
    scores = jnp.einsum('qhgd,chd->hgqc', query_blk.astype(jnp.float32), key_blk.astype(jnp.float32)) * scale
    scores = jnp.where(visible[None, None], scores, -jnp.inf)
    top_score = lax.optimization_barrier(jnp.max(scores, axis=-1, keepdims=True))
    expd = jnp.exp(scores - top_score)
    probs = expd / lax.optimization_barrier(jnp.sum(expd, axis=-1, keepdims=True))
    probs_b = probs.astype(jnp.bfloat16)
    dprobs = jnp.einsum('qhgd,chd->hgqc', dattn_blk.astype(jnp.float32), value_blk.astype(jnp.float32))
    delta = lax.optimization_barrier(jnp.sum(probs * dprobs, axis=-1, keepdims=True))
    dscores = (probs * (dprobs - delta)).astype(jnp.bfloat16)
    dquery = jnp.einsum('hgqc,chd->qhgd', dscores.astype(jnp.float32), key_blk.astype(jnp.float32)) * scale
    dkey = jnp.einsum('hgqc,qhgd->chd', dscores.astype(jnp.float32), query_blk.astype(jnp.float32)) * scale
    value_grad = jnp.einsum('hgqc,qhgd->chd', probs_b.astype(jnp.float32), dattn_blk.astype(jnp.float32))
    return (dquery, dkey, value_grad)

def reference(layer_input, grad_out, doc_start, w_query, key_weight, value_weight, w_out, q_gain, key_norm_gain):
    token_count = layer_input.shape[0]
    token_index = jnp.arange(token_count, dtype=jnp.int32)
    token_positions = token_index - doc_start
    query_raw = jnp.dot(layer_input, w_query, preferred_element_type=jnp.float32)
    key_unrotated = jnp.dot(layer_input, key_weight, preferred_element_type=jnp.float32)
    value_row_matrix = jnp.dot(layer_input, value_weight, preferred_element_type=jnp.float32).astype(jnp.bfloat16)
    query_full, query_back = jax.vjp(lambda unrotated_rows: rotary_normed(unrotated_rows, q_gain, token_positions, QUERY_HEADS), query_raw)
    key_complete, key_backward = jax.vjp(lambda unrotated_rows: rotary_normed(unrotated_rows, key_norm_gain, token_positions, KEY_VALUE_HEADS), key_unrotated)
    query_row_matrix = query_full.astype(jnp.bfloat16)
    key_row_matrix = key_complete.astype(jnp.bfloat16)
    attention_grad = lax.dot_general(grad_out, w_out, (((1,), (1,)), ((), ())), preferred_element_type=jnp.float32).astype(jnp.bfloat16)
    group_width = QUERY_HEADS // KEY_VALUE_HEADS
    query_four_axes = query_row_matrix.reshape(token_count, KEY_VALUE_HEADS, group_width, HEAD_SIZE)
    attention_grad_four = attention_grad.reshape(token_count, KEY_VALUE_HEADS, group_width, HEAD_SIZE)
    window_border = REACH * TOK_DEV
    context_len = (REACH + 1) * TOK_DEV
    key_padded = jnp.concatenate([jnp.zeros((window_border, KEY_VALUE_HEADS, HEAD_SIZE), jnp.bfloat16), key_row_matrix], axis=0)
    value_padded = jnp.concatenate([jnp.zeros((window_border, KEY_VALUE_HEADS, HEAD_SIZE), jnp.bfloat16), value_row_matrix.reshape(token_count, KEY_VALUE_HEADS, HEAD_SIZE)], axis=0)

    def one_block(carry, block_id):
        dkey_pad, value_grad_padded = carry
        start = (block_id * TOK_DEV).astype(jnp.int32)
        query_blk = lax.dynamic_slice_in_dim(query_four_axes, start, TOK_DEV, 0)
        dattn_blk = lax.dynamic_slice_in_dim(attention_grad_four, start, TOK_DEV, 0)
        key_blk = lax.dynamic_slice_in_dim(key_padded, start, context_len, 0)
        value_blk = lax.dynamic_slice_in_dim(value_padded, start, context_len, 0)
        starts_blk = lax.dynamic_slice_in_dim(doc_start, start, TOK_DEV, 0)
        query_ids = start + jnp.arange(TOK_DEV, dtype=jnp.int32)
        key_ids = start - window_border + jnp.arange(context_len, dtype=jnp.int32)
        visible = (key_ids[None, :] >= starts_blk[:, None]) & (key_ids[None, :] <= query_ids[:, None]) & (query_ids[:, None] - key_ids[None, :] < WINDOW)
        dquery, dkey, value_grad = attend(query_blk, key_blk, value_blk, dattn_blk, visible)
        dkey_pad = lax.dynamic_update_slice_in_dim(dkey_pad, lax.dynamic_slice_in_dim(dkey_pad, start, context_len, 0) + dkey, start, 0)
        value_grad_padded = lax.dynamic_update_slice_in_dim(value_grad_padded, lax.dynamic_slice_in_dim(value_grad_padded, start, context_len, 0) + value_grad, start, 0)
        return ((dkey_pad, value_grad_padded), dquery)
    blank_padding = jnp.zeros((window_border + token_count, KEY_VALUE_HEADS, HEAD_SIZE), jnp.float32)
    (dkey_pad, value_grad_padded), dquery_blocks = lax.scan(one_block, (blank_padding, blank_padding), jnp.arange(token_count // TOK_DEV, dtype=jnp.int32))
    dquery = dquery_blocks.reshape(token_count, QUERY_HEADS, HEAD_SIZE)
    dkey = dkey_pad[window_border:]
    value_grad = value_grad_padded[window_border:].reshape(token_count, KEY_VALUE_HEADS * HEAD_SIZE)
    dquery_raw = query_back(dquery)[0].astype(jnp.bfloat16)
    dkey_raw = key_backward(dkey)[0].astype(jnp.bfloat16)
    dvalue_rows = value_grad.astype(jnp.bfloat16)
    contract = (((1,), (1,)), ((), ()))
    grad_input = lax.dot_general(dquery_raw, w_query, contract, preferred_element_type=jnp.float32)
    grad_input = grad_input + lax.dot_general(dkey_raw, key_weight, contract, preferred_element_type=jnp.float32)
    grad_input = grad_input + lax.dot_general(dvalue_rows, value_weight, contract, preferred_element_type=jnp.float32)
    squares = jnp.square(layer_input.astype(jnp.float32))
    fisher_value = lax.dot_general(squares, value_grad * value_grad, (((0,), (0,)), ((), ())), precision=lax.Precision.HIGHEST, preferred_element_type=jnp.float32) / token_count
    return (fisher_value, grad_input.astype(jnp.bfloat16))
```

```python
import math

import jax
import jax.numpy as jnp
from jax import lax
from jax.experimental import pallas as pl
from jax.experimental.pallas import tpu as pltpu
from jax.sharding import PartitionSpec as P

HEAD_SIZE = 128
QSCALE = 168
WINDOW = 1024
NH, NZ, NY, NHEAD = 2, 16, 4, 4
SEQ = NH * NZ * NY
TOK = 128
WIDTH = 2688
ROWS = WIDTH // SEQ
SLOT = 64
FSLOT = 48
GROUP = 16
SPAN = GROUP * ROWS
WIN = 512
F32 = jnp.float32
BF16 = jnp.bfloat16


def dot(a, b, ca=1, cb=0):
    return lax.dot_general(a, b, (((ca,), (cb,)), ((), ())), preferred_element_type=F32)


def iota(shape, axis):
    return lax.broadcasted_iota(jnp.int32, shape, axis)


def rotary(normed, cosine, sine):
    return normed * cosine + pltpu.roll(normed, HEAD_SIZE // 2, 1) * sine


def norm_forward(raw, gain, cosine, sine):
    inv = lax.rsqrt(jnp.mean(raw * raw, axis=1, keepdims=True) + 1e-06)
    return rotary(raw * inv * gain, cosine, sine)


def norm_backward(grad, raw, gain, cosine, sine):
    inv = lax.rsqrt(jnp.mean(raw * raw, axis=1, keepdims=True) + 1e-06)
    back = (grad * cosine + pltpu.roll(grad * sine, HEAD_SIZE // 2, 1)) * gain
    along = jnp.mean(raw * back, axis=1, keepdims=True)
    return inv * (back - raw * (inv * inv * along))


def body(
    piece, x_ref, g_ref, start_ref, cos_ref, sin_ref, qg_ref, kg_ref,
    gi_ref, fv_ref,
    full, lhs, acc, ctx, dctx, ret, tree, treeback, qn, dqn, total, parts, arrived,
    fpad, fone, ftwo, fsend, fy, zsend, zrecv, hsend, hrecv, kvraw,
    send_sem, recv_sem, local_sem,
):
    s = lax.axis_index("seq")
    hd = lax.axis_index("head")
    h = s // (NZ * NY)
    z = lax.rem(s // NY, NZ)
    y = lax.rem(s, NY)
    base = h * (NZ * NY)

    def at_z(step):
        return base + lax.rem(z + step + NZ, NZ) * NY + y

    def at_y(step):
        return base + z * NY + lax.rem(y + step + NY, NY)

    def shifted(step):
        return lax.rem(s + step + SEQ, SEQ)

    zi = lambda step: lax.rem(z + step + 2 * NZ, NZ)
    yi = lambda step: lax.rem(y + step + NY, NY)
    across = (1 - h) * (NZ * NY) + z * NY + y

    barrier = pltpu.get_barrier_semaphore()
    seq_partners = [at_z(1), at_z(-1), at_y(1), at_y(2), at_y(3), across]
    seq_partners += [shifted(4), shifted(-4), shifted(8), shifted(-8)]
    for partner in seq_partners:
        pl.semaphore_signal(barrier, inc=1, device_id={"seq": partner})
    for e in range(1, NHEAD):
        pl.semaphore_signal(barrier, inc=1, device_id={"head": lax.rem(hd + e, NHEAD)})
    pl.semaphore_wait(barrier, len(seq_partners) + NHEAD - 1)

    def remote(src, dst, sem, target, axis="seq"):
        return pltpu.make_async_remote_copy(
            src_ref=src,
            dst_ref=dst,
            send_sem=send_sem.at[sem],
            recv_sem=recv_sem.at[sem],
            device_id={axis: target},
        )

    def here(dst, sem):
        return remote(dst, dst, sem, across)

    HX = 0
    AZ = 1
    BZ = AZ + 16
    AY = BZ + 16
    BY = AY + 64
    KV = BY + 4
    DK = KV + 8
    GR = DK + 8
    FY = GR + 3
    FZ = FY + 6
    FH = FZ + 16

    def rows(lo, n):
        return pl.ds(lo, n)

    def a_piece(zz, yy, lo, n):
        return full.at[:, zz, yy, rows(lo, n), :]

    def b_piece(zz, lo, n):
        return full.at[:, zz, :, rows(lo, n), :]

    def az(k, side, last=False):
        zz = zi(-(k - 1)) if side == 0 else zi(k - 1)
        ref = a_piece(zz, y, 16 * side if last else 0, 16 if last else 32)
        return remote(ref, ref, AZ + 2 * (k - 1) + side, at_z(1 if side == 0 else -1))

    def az_in(k, side, last=False):
        zz = zi(-k) if side == 0 else zi(k)
        ref = a_piece(zz, y, 16 * side if last else 0, 16 if last else 32)
        return here(ref, AZ + 2 * (k - 1) + side)

    def bz(k, side, last=False):
        zz = zi(-(k - 1)) if side == 0 else zi(k - 1)
        ref = b_piece(zz, 32 + 16 * side if last else 32, 16 if last else 32)
        return remote(ref, ref, BZ + 2 * (k - 1) + side, at_z(1 if side == 0 else -1))

    def bz_in(k, side, last=False):
        zz = zi(-k) if side == 0 else zi(k)
        ref = b_piece(zz, 32 + 16 * side if last else 32, 16 if last else 32)
        return here(ref, BZ + 2 * (k - 1) + side)

    def ring_y(zz, sem, lo):
        own = a_piece(zz, y, lo, 32)
        first = [
            remote(own, own, sem, at_y(1)),
            remote(own, own, sem + 1, at_y(3)),
        ]
        left, right, far = yi(3), yi(1), yi(2)
        first_in = [
            here(a_piece(zz, left, lo, 32), sem),
            here(a_piece(zz, right, lo, 32), sem + 1),
        ]
        up = a_piece(zz, left, lo, 16)
        down = a_piece(zz, right, lo + 16, 16)
        second = [
            remote(up, up, sem + 2, at_y(1)),
            remote(down, down, sem + 3, at_y(3)),
        ]
        second_in = [
            here(a_piece(zz, far, lo, 16), sem + 2),
            here(a_piece(zz, far, lo + 16, 16), sem + 3),
        ]
        return first, first_in, second, second_in

    def ay(step, index):
        return ring_y(zi(step), AY + 4 * index, 0)

    def ay_start(step, index):
        for copy in ay(step, index)[0]:
            copy.start()

    def ay_forward(step, index):
        first, first_in, second, second_in = ay(step, index)
        for side in range(2):
            first_in[side].wait_recv()
            second[side].start()

    def ay_finish(step, index):
        first, first_in, second, second_in = ay(step, index)
        for side in range(2):
            second_in[side].wait_recv()
            first[side].wait_send()
            second[side].wait_send()

    own_slot = full.at[h, z, y]
    cross = remote(piece, own_slot, HX, across)
    cross.start()
    keep = pltpu.make_async_copy(piece, own_slot, local_sem.at[0])
    keep.start()
    keep.wait()
    here(full.at[1 - h, z, y], HX).wait_recv()

    b_first, b_first_in, b_second, b_second_in = ring_y(z, BY, 32)
    for side in range(2):
        b_first[side].start()
    for side in range(2):
        az(1, side).start()
    ay_start(0, 0)
    for side in range(2):
        b_first_in[side].wait_recv()
        b_second[side].start()

    def selection(j):
        first_row = SPAN * j
        low = jnp.minimum((first_row // 128) * 128, WIDTH - WIN)
        return pl.multiple_of(low, 128), first_row - low

    def prepare(j):
        low, offset = selection(j)
        column = iota((1, GROUP * SLOT), 1)
        slot = column & (SLOT - 1)
        target = jnp.where(slot < ROWS, offset + (column >> 6) * ROWS + slot, -1)
        select = jnp.where(iota((WIN, GROUP * SLOT), 0) == target, 1.0, 0.0).astype(BF16)
        spread = dot(x_ref[:, pl.ds(low, WIN)], select)
        lhs[j, 0:TOK] = spread.astype(BF16)
        lhs[j, TOK : 2 * TOK] = pltpu.roll(spread, ROWS, 1).astype(BF16)
        spread = dot(g_ref[:, pl.ds(low, WIN)], select)
        lhs[j, 2 * TOK :] = pltpu.roll(spread, 2 * ROWS, 1).astype(BF16)

    prepare(0)
    for side in range(2):
        b_second_in[side].wait_recv()
    for side in range(2):
        bz(1, side).start()

    def step_of(k, last_z, last_next):
        for side in range(2):
            az_in(k, side, last_z).wait_recv()
            if not last_z:
                az(k + 1, side, last_next).start()
        if last_z:
            ay_start(8, 15)
        else:
            ay_start(-k, 2 * k - 1)
            ay_start(k, 2 * k)
        for side in range(2):
            bz_in(k, side, last_z).wait_recv()
            if not last_z:
                bz(k + 1, side, last_next).start()

    step_of(1, False, False)
    ay_forward(0, 0)
    prepare(1)

    def steps(k, carry):
        step_of(k, False, False)
        ay_forward(1 - k, 2 * k - 3)
        ay_forward(k - 1, 2 * k - 2)
        prepare(k)
        return carry

    lax.fori_loop(2, 7, steps, 0)
    step_of(7, False, True)
    ay_forward(-6, 11)
    ay_forward(6, 12)
    prepare(7)
    step_of(8, True, True)
    ay_forward(-7, 13)
    ay_forward(7, 14)
    ay_forward(8, 15)

    cross.wait_send()
    for side in range(2):
        b_first[side].wait_send()
        b_second[side].wait_send()
    for k in range(1, 9):
        for side in range(2):
            az(k, side, k == 8).wait_send()
            bz(k, side, k == 8).wait_send()
    ay_finish(0, 0)

    def finish(k, carry):
        ay_finish(-k, 2 * k - 1)
        ay_finish(k, 2 * k)
        return carry

    lax.fori_loop(1, 8, finish, 0)
    ay_finish(8, 15)

    def weights(j):
        return full[j // 4, pl.ds(4 * lax.rem(j, 4), 4)].reshape(GROUP * SLOT, 512)

    acc[...] = jnp.zeros_like(acc)

    def project(j, carry):
        acc[...] += dot(lhs[j], weights(j))
        return carry

    lax.fori_loop(0, SEQ // GROUP, project, 0)

    cosine, sine = cos_ref[...], sin_ref[...]
    q_gain, k_gain = qg_ref[...], kg_ref[...]
    for i in range(2):
        cols = slice(i * 128, (i + 1) * 128)
        ctx[0, 0, :, cols] = norm_forward(acc[0:TOK, cols], k_gain, cosine, sine).astype(BF16)
    ctx[0, 1] = acc[0:TOK, 256:512].astype(BF16)
    for i in range(4):
        cols = slice(i * 128, (i + 1) * 128)
        qn[i // 2, (i % 2) * TOK : (i % 2 + 1) * TOK] = norm_forward(
            acc[TOK : 2 * TOK, cols], q_gain, cosine, sine
        ).astype(BF16)

    hop4 = remote(ctx.at[0], ctx.at[4], KV, shifted(4))
    hop8 = remote(ctx.at[0], ctx.at[8], KV + 1, shifted(8))
    hop4.start()
    hop8.start()

    def side_copies(e):
        low = jnp.where(y + e < NY, 0, 4)
        one = remote(ctx.at[low], ctx.at[e], KV + 2 * e, at_y(e))
        two = remote(ctx.at[low + 4], ctx.at[e + 4], KV + 2 * e + 1, at_y(e))
        return one, two

    for e in range(1, NY):
        @pl.when(y + e < NY)
        def _():
            side_copies(e)[0].start()
    for i in range(4):
        cols = slice(i * 128, (i + 1) * 128)
        dqn[i // 2, (i % 2) * TOK : (i % 2 + 1) * TOK] = acc[2 * TOK :, cols].astype(BF16)
    here(ctx.at[4], KV).wait_recv()
    for e in range(1, NY):
        @pl.when(y + e < NY)
        def _():
            side_copies(e)[1].start()

        @pl.when(y + e >= NY)
        def _():
            side_copies(e)[0].start()
    here(ctx.at[8], KV + 1).wait_recv()
    for e in range(1, NY):
        @pl.when(y + e >= NY)
        def _():
            side_copies(e)[1].start()
    for e in range(1, NY):
        here(ctx.at[e], KV + 2 * e).wait_recv()
        here(ctx.at[e + 4], KV + 2 * e + 1).wait_recv()
    hop4.wait_send()
    hop8.wait_send()
    for e in range(1, NY):
        one, two = side_copies(e)
        one.wait_send()
        two.wait_send()

    scale = float(QSCALE) ** (-0.5)
    reach = 9 * TOK
    place = iota((reach, 1), 0)
    key_index = s * TOK - (place & ~(TOK - 1)) + (place & (TOK - 1))
    query_index = s * TOK + (iota((1, 2 * TOK), 1) & (TOK - 1))
    visible = (
        (key_index >= start_ref[...])
        & (key_index <= query_index)
        & (query_index - key_index < WINDOW)
    )
    for i in range(2):
        cols = slice(i * 128, (i + 1) * 128)
        keys = ctx[:, 0, :, cols].reshape(reach, 128)
        values = ctx[:, 1, :, cols].reshape(reach, 128)
        queries, douts = qn[i], dqn[i]
        scores = jnp.where(visible, dot(keys, queries, 1, 1) * scale, -jnp.inf)
        expd = jnp.exp(scores - jnp.max(scores, axis=0, keepdims=True))
        probs = expd * (1.0 / jnp.sum(expd, axis=0, keepdims=True))
        dprobs = dot(values, douts, 1, 1)
        delta = jnp.sum(probs * dprobs, axis=0, keepdims=True)
        dscores = (probs * (dprobs - delta)).astype(BF16)
        dctx[:, 0, :, cols] = (dot(dscores, queries) * scale).astype(BF16).reshape(9, TOK, 128)
        dctx[:, 1, :, cols] = dot(probs.astype(BF16), douts).astype(BF16).reshape(9, TOK, 128)
        dquery = dot(dscores, keys, 0, 0) * scale
        for r in range(2):
            col = slice((2 * i + r) * 128, (2 * i + r + 1) * 128)
            kvraw[0, :, col] = norm_backward(
                dquery[r * TOK : (r + 1) * TOK], acc[TOK : 2 * TOK, col], q_gain, cosine, sine
            ).astype(BF16)

    for e in range(1, NY):
        remote(dctx.at[e], ret.at[e - 1, 0], DK + 2 * e, at_y(NY - e)).start()
        remote(dctx.at[e + 4], ret.at[e - 1, 1], DK + 2 * e + 1, at_y(NY - e)).start()

    total[...] = jnp.zeros_like(total)

    def spread_back(which):
        low_slot = ROWS if which == 0 else 0

        def run(j, carry):
            low, offset = selection(j)
            out = dot(kvraw[which], weights(j), 1, 1).astype(BF16)
            row = iota((GROUP * SLOT, 1), 0)
            slot = (row & (SLOT - 1)) - low_slot
            target = jnp.where(
                (slot >= 0) & (slot < ROWS), offset + (row >> 6) * ROWS + slot, -1
            )
            select = jnp.where(iota((GROUP * SLOT, WIN), 1) == target, 1.0, 0.0).astype(BF16)
            total[:, pl.ds(low, WIN)] += dot(out, select)
            return carry

        lax.fori_loop(0, SEQ // GROUP, run, 0)

    sums = [dctx[4 * i].astype(F32) for i in range(3)]
    for e in range(1, NY):
        here(ret.at[e - 1, 0], DK + 2 * e).wait_recv()
        here(ret.at[e - 1, 1], DK + 2 * e + 1).wait_recv()
        same = y + e < NY
        one = ret[e - 1, 0].astype(F32)
        two = ret[e - 1, 1].astype(F32)
        sums[0] += jnp.where(same, one, 0.0)
        sums[1] += jnp.where(same, two, one)
        sums[2] += jnp.where(same, 0.0, two)
    tree[0] = sums[1].astype(BF16)
    tree[1] = sums[2].astype(BF16)
    back4 = remote(tree.at[0], treeback.at[0], DK, shifted(-4))
    back8 = remote(tree.at[1], treeback.at[1], DK + 1, shifted(-8))
    back4.start()
    back8.start()
    kvown = sums[0]
    spread_back(0)
    here(treeback.at[0], DK).wait_recv()
    here(treeback.at[1], DK + 1).wait_recv()
    kvgrad = kvown + treeback[0].astype(F32) + treeback[1].astype(F32)
    back4.wait_send()
    back8.wait_send()
    for e in range(1, NY):
        remote(dctx.at[e], ret.at[e - 1, 0], DK + 2 * e, at_y(NY - e)).wait_send()
        remote(dctx.at[e + 4], ret.at[e - 1, 1], DK + 2 * e + 1, at_y(NY - e)).wait_send()
    dvalue = kvgrad[1]

    place = iota((FSLOT, SPAN), 1)
    slot = iota((FSLOT, SPAN), 0)
    rank = jnp.where(slot < ROWS, slot, jnp.where(slot < 2 * ROWS, slot - ROWS, -WIDTH))
    select = jnp.concatenate(
        [jnp.where(place == rank + ROWS * i, 1.0, 0.0).astype(BF16) for i in range(GROUP)], axis=0
    )
    first_cols = jnp.where(iota((GROUP, FSLOT, 128), 1) < ROWS, 1.0, 0.0)
    dv_sq = (dvalue * dvalue).astype(BF16)

    def squares(i, carry):
        block = x_ref[:, pl.ds(pl.multiple_of(i * 384, 128), 384)].astype(F32)
        fone[pl.ds(pl.multiple_of(i * 384, 128), 384)] = dot(
            (block * block).astype(BF16), dv_sq, 0, 0
        ).astype(BF16)
        return carry

    lax.fori_loop(0, WIDTH // 384, squares, 0)

    def slots(j, carry):
        both = dot(select, fone[pl.ds(pl.multiple_of(SPAN * j, 16), SPAN)])
        both = both.reshape(GROUP, FSLOT, 256)
        picked = jnp.where(first_cols > 0.5, both[:, :, 0:128], both[:, :, 128:256])
        fpad[j // 4, pl.ds(4 * lax.rem(j, 4), 4)] = picked.astype(BF16).reshape(4, 4, FSLOT, 128)
        return carry

    lax.fori_loop(0, SEQ // GROUP, slots, 0)

    far, right, left = yi(2), yi(1), yi(3)
    f1 = remote(fpad.at[0, :, far], ftwo.at[0], FY, at_y(1))
    f2 = remote(fpad.at[1, :, far], ftwo.at[1], FY + 1, at_y(3))
    f3 = remote(fpad.at[1, :, right], ftwo.at[2], FY + 2, at_y(1))
    f4 = remote(fpad.at[0, :, left], ftwo.at[3], FY + 3, at_y(3))
    for copy in (f1, f2, f3, f4):
        copy.start()

    for i in range(2):
        cols = slice(i * 128, (i + 1) * 128)
        kvraw[1, :, cols] = norm_backward(
            kvgrad[0, :, cols], acc[0:TOK, cols], k_gain, cosine, sine
        ).astype(BF16)
    kvraw[1, :, 256:512] = dvalue.astype(BF16)

    here(ftwo.at[0], FY).wait_recv()
    fsend[0] = (fpad[0, :, right].astype(F32) + ftwo[0].astype(F32)).astype(BF16)
    f5 = remote(fsend.at[0], ftwo.at[4], FY + 4, at_y(1))
    f5.start()
    here(ftwo.at[1], FY + 1).wait_recv()
    fsend[1] = (fpad[1, :, left].astype(F32) + ftwo[1].astype(F32)).astype(BF16)
    f6 = remote(fsend.at[1], ftwo.at[5], FY + 5, at_y(3))
    f6.start()

    spread_back(1)
    for i in range(NHEAD):
        parts[i] = total[i * 32 : (i + 1) * 32].astype(BF16)
    shares = []
    for e in range(1, NHEAD):
        to = lax.rem(hd + e, NHEAD)
        shares.append(remote(parts.at[to], arrived.at[e - 1], GR + e - 1, to, "head"))
        shares[-1].start()

    for i in range(2, 6):
        here(ftwo.at[i], FY + i).wait_recv()
    fy[0] = fpad[0, :, y].astype(F32) + ftwo[4].astype(F32) + ftwo[3].astype(F32)
    fy[1] = fpad[1, :, y].astype(F32) + ftwo[2].astype(F32) + ftwo[5].astype(F32)

    def fz(k, side, first=False):
        i = 2 * (k - 1) + side
        src, dst = zsend.at[i], zrecv.at[i]
        if first:
            src, dst = src.at[side], dst.at[side]
        return remote(src, dst, FZ + i, at_z(1 if side == 0 else -1))

    def fz_in(k, side, first=False):
        i = 2 * (k - 1) + side
        return here(zrecv.at[i].at[side] if first else zrecv.at[i], FZ + i)

    for side in range(2):
        zsend[side, side] = fy[side, zi(8)].astype(BF16)
        fz(1, side, True).start()
    for k in range(1, 8):
        for side in range(2):
            fz_in(k, side, k == 1).wait_recv()
            i = 2 * (k - 1) + side
            own = zi(8 - k) if side == 0 else zi(k - 8)
            for part in range(2):
                value = fy[part, own]
                if k > 1 or part == side:
                    value = value + zrecv[i, part].astype(F32)
                zsend[i + 2, part] = value.astype(BF16)
            fz(k + 1, side).start()
    for side in range(2):
        fz_in(8, side).wait_recv()
    sums = [fy[p, z] + zrecv[14, p].astype(F32) + zrecv[15, p].astype(F32) for p in range(2)]
    low_half = h == 0
    hsend[...] = jnp.where(low_half, sums[1], sums[0]).astype(BF16)
    last = remote(hsend, hrecv, FH, across)
    last.start()

    for e in range(1, NHEAD):
        here(arrived.at[e - 1], GR + e - 1).wait_recv()
    mine = total[pl.ds(pl.multiple_of(hd * 32, 32), 32)]
    for e in range(1, NHEAD):
        mine = mine + arrived[e - 1].astype(F32)
    gi_ref[...] = mine.astype(BF16)
    for copy in shares:
        copy.wait_send()

    here(hrecv, FH).wait_recv()
    fv_ref[...] = (jnp.where(low_half, sums[0], sums[1]) + hrecv[...].astype(F32)) * (
        1.0 / (SEQ * TOK)
    )
    last.wait_send()
    for copy in (f1, f2, f3, f4, f5, f6):
        copy.wait_send()
    for k in range(1, 9):
        for side in range(2):
            fz(k, side, k == 1).wait_send()


def layer(piece, x, g, starts, cosine, sine, q_gain, k_gain):
    vmem = pl.BlockSpec(memory_space=pltpu.VMEM)
    sems = 160
    return pl.pallas_call(
        body,
        name="layer_backward",
        out_shape=(
            jax.ShapeDtypeStruct((32, WIDTH), BF16),
            jax.ShapeDtypeStruct((FSLOT, 128), F32),
        ),
        in_specs=[pl.BlockSpec(memory_space=pl.ANY)] + [vmem] * 7,
        out_specs=(vmem, vmem),
        scratch_shapes=[
            pltpu.VMEM((NH, NZ, NY, SLOT, 512), BF16),
            pltpu.VMEM((SEQ // GROUP, 3 * TOK, GROUP * SLOT), BF16),
            pltpu.VMEM((3 * TOK, 512), F32),
            pltpu.VMEM((9, 2, TOK, 256), BF16),
            pltpu.VMEM((9, 2, TOK, 256), BF16),
            pltpu.VMEM((3, 2, 2, TOK, 256), BF16),
            pltpu.VMEM((2, 2, TOK, 256), BF16),
            pltpu.VMEM((2, 2, TOK, 256), BF16),
            pltpu.VMEM((2, 2 * TOK, 128), BF16),
            pltpu.VMEM((2, 2 * TOK, 128), BF16),
            pltpu.VMEM((TOK, WIDTH), F32),
            pltpu.VMEM((NHEAD, 32, WIDTH), BF16),
            pltpu.VMEM((NHEAD - 1, 32, WIDTH), BF16),
            pltpu.VMEM((NH, NZ, NY, FSLOT, 128), BF16),
            pltpu.VMEM((WIDTH, 256), BF16),
            pltpu.VMEM((6, NZ, FSLOT, 128), BF16),
            pltpu.VMEM((2, NZ, FSLOT, 128), BF16),
            pltpu.VMEM((NH, NZ, FSLOT, 128), F32),
            pltpu.VMEM((16, NH, FSLOT, 128), BF16),
            pltpu.VMEM((16, NH, FSLOT, 128), BF16),
            pltpu.VMEM((FSLOT, 128), BF16),
            pltpu.VMEM((FSLOT, 128), BF16),
            pltpu.VMEM((2, TOK, 512), BF16),
            pltpu.SemaphoreType.DMA((sems,)),
            pltpu.SemaphoreType.DMA((sems,)),
            pltpu.SemaphoreType.DMA((1,)),
        ],
        compiler_params=pltpu.CompilerParams(
            collective_id=0, has_side_effects=True, vmem_limit_bytes=60 * 1024 * 1024
        ),
    )(piece, x, g, starts, cosine, sine, q_gain, k_gain)


def on_device(
    layer_input,
    grad_out,
    doc_start,
    w_query,
    key_weight,
    value_weight,
    w_out,
    q_gain,
    key_norm_gain,
):
    seq_index = lax.axis_index("seq")
    token_index = seq_index * TOK + jnp.arange(TOK, dtype=jnp.int32)
    positions = (token_index - doc_start).astype(F32)
    half = HEAD_SIZE // 2
    frequency = jnp.exp(jnp.arange(half).astype(F32) * (-math.log(10000.0) / half))
    angles = positions[:, None] * frequency[None, :]
    cosine, sine = jnp.cos(angles), jnp.sin(angles)
    cosine = jnp.concatenate([cosine, cosine], axis=1)
    sine = jnp.concatenate([-sine, sine], axis=1)
    piece = jnp.concatenate(
        [
            jnp.concatenate([key_weight, value_weight], axis=1),
            w_query,
            w_out.T,
            jnp.zeros((1, 512), BF16),
        ],
        axis=0,
    )
    starts = jnp.concatenate([doc_start, doc_start])[None, :]
    grad_input, sums = layer(
        piece, layer_input, grad_out, starts, cosine, sine, q_gain[None, :], key_norm_gain[None, :]
    )
    fisher_value = jnp.concatenate([sums[0:ROWS], sums[ROWS : 2 * ROWS]], axis=1)
    return (fisher_value, grad_input)


def solution(mesh):
    in_specs = (
        P("seq", None),
        P("seq", None),
        P("seq"),
        P("seq", "head"),
        P("seq", "head"),
        P("seq", "head"),
        P("head", "seq"),
        P(),
        P(),
    )
    out_specs = (P("seq", "head"), P(("seq", "head"), None))
    return jax.shard_map(
        on_device, mesh=mesh, in_specs=in_specs, out_specs=out_specs, check_vma=False
    )
```

```python
import math

import jax
import jax.numpy as jnp
from jax import lax
from jax.experimental import pallas as pl
from jax.experimental.pallas import tpu as pltpu
from jax.sharding import PartitionSpec as P

HEAD_SIZE = 128
QSCALE = 168
WINDOW = 1024
NH, NZ, NY, NHEAD = 2, 16, 4, 4
SEQ = NH * NZ * NY
TOK = 128
WIDTH = 2688
ROWS = WIDTH // SEQ
SLOT = 64
FSLOT = 48
GROUP = 16
SPAN = GROUP * ROWS
WIN = 512
F32 = jnp.float32
BF16 = jnp.bfloat16


def dot(a, b, ca=1, cb=0):
    return lax.dot_general(a, b, (((ca,), (cb,)), ((), ())), preferred_element_type=F32)


def iota(shape, axis):
    return lax.broadcasted_iota(jnp.int32, shape, axis)


def rotary(normed, cosine, sine):
    return normed * cosine + pltpu.roll(normed, HEAD_SIZE // 2, 1) * sine


def norm_forward(raw, gain, cosine, sine):
    inv = lax.rsqrt(jnp.mean(raw * raw, axis=1, keepdims=True) + 1e-06)
    return rotary(raw * inv * gain, cosine, sine)


def norm_backward(grad, raw, gain, cosine, sine):
    inv = lax.rsqrt(jnp.mean(raw * raw, axis=1, keepdims=True) + 1e-06)
    back = (grad * cosine + pltpu.roll(grad * sine, HEAD_SIZE // 2, 1)) * gain
    along = jnp.mean(raw * back, axis=1, keepdims=True)
    return inv * (back - raw * (inv * inv * along))


def body(
    piece, x_ref, g_ref, start_ref, cos_ref, sin_ref, qg_ref, kg_ref,
    gi_ref, fv_ref,
    full, lhs, acc, ctx, dctx, ret, tree, treeback, qn, dqn, total, parts, arrived,
    fpad, fone, ftwo, fsend, fy, flow, fmid, flo, flsend, usend, urecv, last, zsend, zrecv,
    kvraw,
    send_sem, recv_sem, local_sem,
):
    s = lax.axis_index("seq")
    hd = lax.axis_index("head")
    h = s // (NZ * NY)
    z = lax.rem(s // NY, NZ)
    y = lax.rem(s, NY)
    base = h * (NZ * NY)

    def at_z(step):
        return base + lax.rem(z + step + NZ, NZ) * NY + y

    def at_y(step):
        return base + z * NY + lax.rem(y + step + NY, NY)

    def shifted(step):
        return lax.rem(s + step + SEQ, SEQ)

    zi = lambda step: lax.rem(z + step + 2 * NZ, NZ)
    yi = lambda step: lax.rem(y + step + NY, NY)
    across = (1 - h) * (NZ * NY) + z * NY + y

    barrier = pltpu.get_barrier_semaphore()
    seq_partners = [at_z(1), at_z(-1), at_y(1), at_y(2), at_y(3), across]
    seq_partners += [shifted(4), shifted(-4), shifted(8), shifted(-8)]
    for partner in seq_partners:
        pl.semaphore_signal(barrier, inc=1, device_id={"seq": partner})
    for e in range(1, NHEAD):
        pl.semaphore_signal(barrier, inc=1, device_id={"head": lax.rem(hd + e, NHEAD)})
    pl.semaphore_wait(barrier, len(seq_partners) + NHEAD - 1)

    def remote(src, dst, sem, target, axis="seq"):
        return pltpu.make_async_remote_copy(
            src_ref=src,
            dst_ref=dst,
            send_sem=send_sem.at[sem],
            recv_sem=recv_sem.at[sem],
            device_id={axis: target},
        )

    def here(dst, sem):
        return remote(dst, dst, sem, across)

    HX = 0
    AZ = HX + 1
    BZ = AZ + 32
    AY = BZ + 32
    BY = AY + 96
    BX = BY + 4
    KV = BX + 16
    DK = KV + 8
    GR = DK + 16
    FY = GR + 3
    FL = FY + 6
    FH = FL + 6
    FZ = FH + 2

    side_z = lambda side: at_z(1 if side == 0 else -1)
    xs = (h, 1 - h)

    def a_piece(c, zz, yy):
        return full.at[xs[c], zz, yy, pl.ds(0, 32), :]

    def b_piece(zz, b):
        return full.at[h, zz, :, pl.ds(32 + 16 * b, 16), :]

    def az(c, k, side):
        ref = a_piece(c, zi(1 - k) if side == 0 else zi(k - 1), y)
        return remote(ref, ref, AZ + 16 * c + 2 * (k - 1) + side, side_z(side))

    def az_in(c, k, side):
        ref = a_piece(c, zi(-k) if side == 0 else zi(k), y)
        return here(ref, AZ + 16 * c + 2 * (k - 1) + side)

    def bz(b, k, side):
        ref = b_piece(zi(1 - k) if side == 0 else zi(k - 1), b)
        return remote(ref, ref, BZ + 16 * b + 2 * (k - 1) + side, side_z(side))

    def bz_in(b, k, side):
        ref = b_piece(zi(-k) if side == 0 else zi(k), b)
        return here(ref, BZ + 16 * b + 2 * (k - 1) + side)

    def bx(step, index):
        ref = full.at[h, zi(step), :, pl.ds(32, 32), :]
        return remote(ref, ref, BX + index, across)

    def bx_in(step, index):
        return here(full.at[1 - h, zi(step), :, pl.ds(32, 32), :], BX + index)

    left, right, far = yi(3), yi(1), yi(2)

    def ay_start(c, step, index):
        sem = AY + 48 * c + 3 * index
        own = a_piece(c, zi(step), y)
        remote(own, own, sem, at_y(1)).start()
        remote(own, own, sem + 1, at_y(3)).start()

    def ay_forward(c, step, index):
        sem = AY + 48 * c + 3 * index
        zz = zi(step)
        here(a_piece(c, zz, left), sem).wait_recv()
        here(a_piece(c, zz, right), sem + 1).wait_recv()
        ref = a_piece(c, zz, right if c else left)
        remote(ref, ref, sem + 2, at_y(3 if c else 1)).start()

    def ay_finish(c, step, index):
        sem = AY + 48 * c + 3 * index
        zz = zi(step)
        here(a_piece(c, zz, far), sem + 2).wait_recv()
        own = a_piece(c, zz, y)
        for i in range(3):
            here(own, sem + i).wait_send()

    own_slot = full.at[h, z, y]
    cross = remote(piece.at[pl.ds(0, 32)], own_slot.at[pl.ds(0, 32)], HX, across)
    cross.start()
    keep = pltpu.make_async_copy(piece, own_slot, local_sem.at[0])
    keep.start()
    keep.wait()

    def by_piece(yy, lo, n):
        return full.at[h, z, yy, pl.ds(lo, n), :]

    mine = by_piece(y, 32, 32)
    by_first = [remote(mine, mine, BY, at_y(1)), remote(mine, mine, BY + 1, at_y(3))]
    for copy in by_first:
        copy.start()
    for side in range(2):
        az(0, 1, side).start()
    ay_start(0, 0, 0)
    here(a_piece(1, z, y), HX).wait_recv()
    for side in range(2):
        az(1, 1, side).start()
    ay_start(1, 0, 0)
    up, down = by_piece(left, 32, 16), by_piece(right, 48, 16)
    by_second = [remote(up, up, BY + 2, at_y(1)), remote(down, down, BY + 3, at_y(3))]
    here(by_piece(left, 32, 32), BY).wait_recv()
    by_second[0].start()
    here(by_piece(right, 32, 32), BY + 1).wait_recv()
    by_second[1].start()
    for i in range(2):
        here(by_piece(far, 32 + 16 * i, 16), BY + 2 + i).wait_recv()
        for side in range(2):
            bz(i, 1, side).start()
    bx(0, 0).start()

    def selection(j):
        first_row = SPAN * j
        low = jnp.minimum((first_row // 128) * 128, WIDTH - WIN)
        return pl.multiple_of(low, 128), first_row - low

    def prepare(j):
        low, offset = selection(j)
        column = iota((1, GROUP * SLOT), 1)
        slot = column & (SLOT - 1)
        target = jnp.where(slot < ROWS, offset + (column >> 6) * ROWS + slot, -1)
        select = jnp.where(iota((WIN, GROUP * SLOT), 0) == target, 1.0, 0.0).astype(BF16)
        spread = dot(x_ref[:, pl.ds(low, WIN)], select)
        lhs[j, 0:TOK] = spread.astype(BF16)
        lhs[j, TOK : 2 * TOK] = pltpu.roll(spread, ROWS, 1).astype(BF16)
        spread = dot(g_ref[:, pl.ds(low, WIN)], select)
        lhs[j, 2 * TOK :] = pltpu.roll(spread, 2 * ROWS, 1).astype(BF16)

    def place_of(k, side):
        return (-k if side == 0 else k), 2 * k - 1 + side

    def step_of(k, final):
        for c in range(2):
            for side in range(2):
                az_in(c, k, side).wait_recv()
                if not final or side == c:
                    az(c, k + 1, side).start()
                ay_start(c, *place_of(k, side))
        for b in range(2):
            for side in range(2):
                bz_in(b, k, side).wait_recv()
                if not final or side == b:
                    bz(b, k + 1, side).start()
        for side in range(2):
            bx(*place_of(k, side)).start()

    def forward_of(k):
        for c in range(2):
            for side in range(2):
                ay_forward(c, *place_of(k, side))

    prepare(0)
    step_of(1, False)
    for c in range(2):
        ay_forward(c, 0, 0)
    prepare(1)

    def steps(k, carry):
        step_of(k, False)
        forward_of(k - 1)
        prepare(k)
        return carry

    lax.fori_loop(2, 7, steps, 0)
    step_of(7, True)
    forward_of(6)
    prepare(7)
    for c in range(2):
        az_in(c, 8, c).wait_recv()
        ay_start(c, 8, 15)
    for b in range(2):
        bz_in(b, 8, b).wait_recv()
    bx(8, 15).start()
    forward_of(7)
    for c in range(2):
        ay_forward(c, 8, 15)

    cross.wait_send()
    for copy in by_first + by_second:
        copy.wait_send()
    for c in range(2):
        ay_finish(c, 0, 0)
    bx_in(0, 0).wait_recv()
    bx(0, 0).wait_send()

    def finish(k, carry):
        for side in range(2):
            for c in range(2):
                az(c, k, side).wait_send()
                bz(c, k, side).wait_send()
                ay_finish(c, *place_of(k, side))
            bx_in(*place_of(k, side)).wait_recv()
            bx(*place_of(k, side)).wait_send()
        return carry

    lax.fori_loop(1, 8, finish, 0)
    for c in range(2):
        az(c, 8, c).wait_send()
        bz(c, 8, c).wait_send()
        ay_finish(c, 8, 15)
    bx_in(8, 15).wait_recv()
    bx(8, 15).wait_send()

    def weights(j):
        return full[j // 4, pl.ds(4 * lax.rem(j, 4), 4)].reshape(GROUP * SLOT, 512)

    acc[...] = jnp.zeros_like(acc)

    def project(j, carry):
        acc[...] += dot(lhs[j], weights(j))
        return carry

    lax.fori_loop(0, SEQ // GROUP, project, 0)

    cosine, sine = cos_ref[...], sin_ref[...]
    q_gain, k_gain = qg_ref[...], kg_ref[...]
    for i in range(2):
        cols = slice(i * 128, (i + 1) * 128)
        ctx[0, 0, :, cols] = norm_forward(acc[0:TOK, cols], k_gain, cosine, sine).astype(BF16)
    ctx[0, 1] = acc[0:TOK, 256:512].astype(BF16)
    for i in range(4):
        cols = slice(i * 128, (i + 1) * 128)
        qn[i // 2, (i % 2) * TOK : (i % 2 + 1) * TOK] = norm_forward(
            acc[TOK : 2 * TOK, cols], q_gain, cosine, sine
        ).astype(BF16)

    hop4 = remote(ctx.at[0], ctx.at[4], KV, shifted(4))
    hop8 = remote(ctx.at[4], ctx.at[8], KV + 1, shifted(4))
    hop4.start()

    def side_copies(e):
        low = jnp.where(y + e < NY, 0, 4)
        one = remote(ctx.at[low], ctx.at[e], KV + 2 * e, at_y(e))
        two = remote(ctx.at[low + 4], ctx.at[e + 4], KV + 2 * e + 1, at_y(e))
        return one, two

    for e in range(1, NY):
        @pl.when(y + e < NY)
        def _():
            side_copies(e)[0].start()
    for i in range(4):
        cols = slice(i * 128, (i + 1) * 128)
        dqn[i // 2, (i % 2) * TOK : (i % 2 + 1) * TOK] = acc[2 * TOK :, cols].astype(BF16)
    here(ctx.at[4], KV).wait_recv()
    hop8.start()
    for e in range(1, NY):
        @pl.when(y + e < NY)
        def _():
            side_copies(e)[1].start()

        @pl.when(y + e >= NY)
        def _():
            side_copies(e)[0].start()
    here(ctx.at[8], KV + 1).wait_recv()
    for e in range(1, NY):
        @pl.when(y + e >= NY)
        def _():
            side_copies(e)[1].start()
    for e in range(1, NY):
        here(ctx.at[e], KV + 2 * e).wait_recv()
        here(ctx.at[e + 4], KV + 2 * e + 1).wait_recv()
    hop4.wait_send()
    hop8.wait_send()
    for e in range(1, NY):
        one, two = side_copies(e)
        one.wait_send()
        two.wait_send()

    scale = float(QSCALE) ** (-0.5)
    reach = 9 * TOK
    place = iota((reach, 1), 0)
    key_index = s * TOK - (place & ~(TOK - 1)) + (place & (TOK - 1))
    query_index = s * TOK + (iota((1, 2 * TOK), 1) & (TOK - 1))
    visible = (
        (key_index >= start_ref[...])
        & (key_index <= query_index)
        & (query_index - key_index < WINDOW)
    )
    for i in range(2):
        cols = slice(i * 128, (i + 1) * 128)
        keys = ctx[:, 0, :, cols].reshape(reach, 128)
        values = ctx[:, 1, :, cols].reshape(reach, 128)
        queries, douts = qn[i], dqn[i]
        scores = jnp.where(visible, dot(keys, queries, 1, 1) * scale, -jnp.inf)
        expd = jnp.exp(scores - jnp.max(scores, axis=0, keepdims=True))
        probs = expd * (1.0 / jnp.sum(expd, axis=0, keepdims=True))
        dprobs = dot(values, douts, 1, 1)
        delta = jnp.sum(probs * dprobs, axis=0, keepdims=True)
        dscores = (probs * (dprobs - delta)).astype(BF16)
        dctx[:, 0, :, cols] = (dot(dscores, queries) * scale).astype(BF16).reshape(9, TOK, 128)
        dctx[:, 1, :, cols] = dot(probs.astype(BF16), douts).astype(BF16).reshape(9, TOK, 128)
        dquery = dot(dscores, keys, 0, 0) * scale
        for r in range(2):
            col = slice((2 * i + r) * 128, (2 * i + r + 1) * 128)
            kvraw[0, :, col] = norm_backward(
                dquery[r * TOK : (r + 1) * TOK], acc[TOK : 2 * TOK, col], q_gain, cosine, sine
            ).astype(BF16)

    def side_back(e, which):
        sem = DK + 6 * which + 2 * (e - 1)
        return [
            remote(dctx.at[e + 4 * i, which], ret.at[e - 1, i, which], sem + i, at_y(NY - e))
            for i in range(2)
        ]

    def tree_back(which):
        sem = DK + 12 + 2 * which
        return [
            remote(tree.at[which, i], treeback.at[which, i], sem + i, shifted(-4 * (i + 1)))
            for i in range(2)
        ]

    for which in (1, 0):
        for e in range(1, NY):
            for copy in side_back(e, which):
                copy.start()

    def gather_sums(which):
        sums = [dctx[4 * i, which].astype(F32) for i in range(3)]
        for e in range(1, NY):
            for i in range(2):
                here(ret.at[e - 1, i, which], DK + 6 * which + 2 * (e - 1) + i).wait_recv()
            same = y + e < NY
            one = ret[e - 1, 0, which].astype(F32)
            two = ret[e - 1, 1, which].astype(F32)
            sums[0] += jnp.where(same, one, 0.0)
            sums[1] += jnp.where(same, two, one)
            sums[2] += jnp.where(same, 0.0, two)
        tree[which, 0] = sums[1].astype(BF16)
        tree[which, 1] = sums[2].astype(BF16)
        for copy in tree_back(which):
            copy.start()
        return sums[0]

    def whole(which, own):
        for i in range(2):
            here(treeback.at[which, i], DK + 12 + 2 * which + i).wait_recv()
            own = own + treeback[which, i].astype(F32)
        return own

    total[...] = jnp.zeros_like(total)

    def spread_back(which, lo, hi):
        low_slot = ROWS if which == 0 else 0

        def run(j, carry):
            low, offset = selection(j)
            out = dot(kvraw[which], weights(j), 1, 1).astype(BF16)
            row = iota((GROUP * SLOT, 1), 0)
            slot = (row & (SLOT - 1)) - low_slot
            target = jnp.where(
                (slot >= 0) & (slot < ROWS), offset + (row >> 6) * ROWS + slot, -1
            )
            select = jnp.where(iota((GROUP * SLOT, WIN), 1) == target, 1.0, 0.0).astype(BF16)
            total[:, pl.ds(low, WIN)] += dot(out, select)
            return carry

        lax.fori_loop(lo, hi, run, 0)

    spread_back(0, 0, 4)
    own_dv = gather_sums(1)
    own_dk = gather_sums(0)
    dvalue = whole(1, own_dv)

    place = iota((FSLOT, SPAN), 1)
    slot = iota((FSLOT, SPAN), 0)
    rank = jnp.where(slot < ROWS, slot, jnp.where(slot < 2 * ROWS, slot - ROWS, -WIDTH))
    select = jnp.concatenate(
        [jnp.where(place == rank + ROWS * i, 1.0, 0.0).astype(BF16) for i in range(GROUP)], axis=0
    )
    first_cols = jnp.where(iota((GROUP, FSLOT, 128), 1) < ROWS, 1.0, 0.0)
    dv_sq = (dvalue * dvalue).astype(BF16)

    def squares(i, carry):
        block = x_ref[:, pl.ds(pl.multiple_of(i * 384, 128), 384)].astype(F32)
        fone[pl.ds(pl.multiple_of(i * 384, 128), 384)] = dot(
            (block * block).astype(BF16), dv_sq, 0, 0
        ).astype(BF16)
        return carry

    lax.fori_loop(0, WIDTH // 384, squares, 0)

    def slots(j, carry):
        both = dot(select, fone[pl.ds(pl.multiple_of(SPAN * j, 16), SPAN)])
        both = both.reshape(GROUP, FSLOT, 256)
        picked = jnp.where(first_cols > 0.5, both[:, :, 0:128], both[:, :, 128:256])
        fpad[j // 4, pl.ds(4 * lax.rem(j, 4), 4)] = picked.astype(BF16).reshape(4, 4, FSLOT, 128)
        return carry

    lax.fori_loop(0, SEQ // GROUP, slots, 0)

    cross_low = remote(fpad.at[1 - h, pl.ds(0, 8)], flow, FH, across)
    cross_low.start()

    def ring(pick, buf, sem):
        return [
            remote(pick(0, far), buf.at[0], sem, at_y(1)),
            remote(pick(1, far), buf.at[1], sem + 1, at_y(3)),
            remote(pick(1, right), buf.at[2], sem + 2, at_y(1)),
            remote(pick(0, left), buf.at[3], sem + 3, at_y(3)),
        ]

    def ring_next(pick_value, buf, send, sem):
        here(buf.at[0], sem).wait_recv()
        send[0] = (pick_value(0, right) + buf[0].astype(F32)).astype(BF16)
        one = remote(send.at[0], buf.at[4], sem + 4, at_y(1))
        one.start()
        here(buf.at[1], sem + 1).wait_recv()
        send[1] = (pick_value(1, left) + buf[1].astype(F32)).astype(BF16)
        two = remote(send.at[1], buf.at[5], sem + 5, at_y(3))
        two.start()
        return [one, two]

    def ring_end(pick_value, buf, sem):
        for i in range(2, 6):
            here(buf.at[i], sem + i).wait_recv()
        first = pick_value(0, y) + buf[4].astype(F32) + buf[3].astype(F32)
        second = pick_value(1, y) + buf[2].astype(F32) + buf[5].astype(F32)
        return first, second

    up_ring = ring(lambda i, yy: fpad.at[i, pl.ds(8, 8), yy], ftwo, FY)
    for copy in up_ring:
        copy.start()
    spread_back(0, 4, 8)
    up_value = lambda i, yy: fpad[i, 8:16, yy].astype(F32)
    up_ring += ring_next(up_value, ftwo, fsend, FY)

    here(flow, FH).wait_recv()
    fmid[...] = (fpad[h, 0:8].astype(F32) + flow[...].astype(F32)).astype(BF16)
    low_ring = ring(lambda i, yy: fmid.at[pl.ds(4 * i, 4), yy], flo, FL)
    for copy in low_ring:
        copy.start()

    dkey = whole(0, own_dk)
    for i in range(2):
        cols = slice(i * 128, (i + 1) * 128)
        kvraw[1, :, cols] = norm_backward(
            dkey[:, cols], acc[0:TOK, cols], k_gain, cosine, sine
        ).astype(BF16)
    kvraw[1, :, 256:512] = dvalue.astype(BF16)
    spread_back(1, 0, 2)

    fy[0], fy[1] = ring_end(up_value, ftwo, FY)
    usend[...] = fy[1 - h].astype(BF16)
    cross_up = remote(usend, urecv, FH + 1, across)
    cross_up.start()
    low_value = lambda i, yy: fmid[4 * i : 4 * i + 4, yy].astype(F32)
    low_ring += ring_next(low_value, flo, flsend, FL)

    spread_back(1, 2, 5)
    last[0:4], last[4:8] = ring_end(low_value, flo, FL)
    here(urecv, FH + 1).wait_recv()
    last[8:16] = fy[h] + urecv[...].astype(F32)
    zsend[...] = last[...].astype(BF16)

    def to_z(d):
        return remote(zsend.at[zi(d)], zrecv.at[d - 1], FZ + d - 1, at_z(d))

    for d in (8, 7, 9, 6, 10, 5, 11, 4, 12, 3, 13, 2, 14, 1, 15):
        to_z(d).start()

    spread_back(1, 5, 8)
    for i in range(NHEAD):
        parts[i] = total[i * 32 : (i + 1) * 32].astype(BF16)
    shares = []
    for e in range(1, NHEAD):
        to = lax.rem(hd + e, NHEAD)
        shares.append(remote(parts.at[to], arrived.at[e - 1], GR + e - 1, to, "head"))
        shares[-1].start()

    sums = last[z]
    for d in range(1, NZ):
        here(zrecv.at[d - 1], FZ + d - 1).wait_recv()
        sums = sums + zrecv[d - 1].astype(F32)
    fv_ref[...] = sums * (1.0 / (SEQ * TOK))

    for e in range(1, NHEAD):
        here(arrived.at[e - 1], GR + e - 1).wait_recv()
    mine = total[pl.ds(pl.multiple_of(hd * 32, 32), 32)]
    for e in range(1, NHEAD):
        mine = mine + arrived[e - 1].astype(F32)
    gi_ref[...] = mine.astype(BF16)

    for copy in shares + up_ring + low_ring + [cross_low, cross_up]:
        copy.wait_send()
    for d in range(1, NZ):
        to_z(d).wait_send()
    for which in range(2):
        for copy in tree_back(which):
            copy.wait_send()
        for e in range(1, NY):
            for copy in side_back(e, which):
                copy.wait_send()


def layer(piece, x, g, starts, cosine, sine, q_gain, k_gain):
    vmem = pl.BlockSpec(memory_space=pltpu.VMEM)
    sems = 256
    return pl.pallas_call(
        body,
        name="layer_backward",
        out_shape=(
            jax.ShapeDtypeStruct((32, WIDTH), BF16),
            jax.ShapeDtypeStruct((FSLOT, 128), F32),
        ),
        in_specs=[pl.BlockSpec(memory_space=pl.ANY)] + [vmem] * 7,
        out_specs=(vmem, vmem),
        scratch_shapes=[
            pltpu.VMEM((NH, NZ, NY, SLOT, 512), BF16),
            pltpu.VMEM((SEQ // GROUP, 3 * TOK, GROUP * SLOT), BF16),
            pltpu.VMEM((3 * TOK, 512), F32),
            pltpu.VMEM((9, 2, TOK, 256), BF16),
            pltpu.VMEM((9, 2, TOK, 256), BF16),
            pltpu.VMEM((3, 2, 2, TOK, 256), BF16),
            pltpu.VMEM((2, 2, TOK, 256), BF16),
            pltpu.VMEM((2, 2, TOK, 256), BF16),
            pltpu.VMEM((2, 2 * TOK, 128), BF16),
            pltpu.VMEM((2, 2 * TOK, 128), BF16),
            pltpu.VMEM((TOK, WIDTH), F32),
            pltpu.VMEM((NHEAD, 32, WIDTH), BF16),
            pltpu.VMEM((NHEAD - 1, 32, WIDTH), BF16),
            pltpu.VMEM((NH, NZ, NY, FSLOT, 128), BF16),
            pltpu.VMEM((WIDTH, 256), BF16),
            pltpu.VMEM((6, 8, FSLOT, 128), BF16),
            pltpu.VMEM((2, 8, FSLOT, 128), BF16),
            pltpu.VMEM((NH, 8, FSLOT, 128), F32),
            pltpu.VMEM((8, NY, FSLOT, 128), BF16),
            pltpu.VMEM((8, NY, FSLOT, 128), BF16),
            pltpu.VMEM((6, 4, FSLOT, 128), BF16),
            pltpu.VMEM((2, 4, FSLOT, 128), BF16),
            pltpu.VMEM((8, FSLOT, 128), BF16),
            pltpu.VMEM((8, FSLOT, 128), BF16),
            pltpu.VMEM((NZ, FSLOT, 128), F32),
            pltpu.VMEM((NZ, FSLOT, 128), BF16),
            pltpu.VMEM((NZ - 1, FSLOT, 128), BF16),
            pltpu.VMEM((2, TOK, 512), BF16),
            pltpu.SemaphoreType.DMA((sems,)),
            pltpu.SemaphoreType.DMA((sems,)),
            pltpu.SemaphoreType.DMA((1,)),
        ],
        compiler_params=pltpu.CompilerParams(
            collective_id=0, has_side_effects=True, vmem_limit_bytes=60 * 1024 * 1024
        ),
    )(piece, x, g, starts, cosine, sine, q_gain, k_gain)


def on_device(
    layer_input,
    grad_out,
    doc_start,
    w_query,
    key_weight,
    value_weight,
    w_out,
    q_gain,
    key_norm_gain,
):
    seq_index = lax.axis_index("seq")
    token_index = seq_index * TOK + jnp.arange(TOK, dtype=jnp.int32)
    positions = (token_index - doc_start).astype(F32)
    half = HEAD_SIZE // 2
    frequency = jnp.exp(jnp.arange(half).astype(F32) * (-math.log(10000.0) / half))
    angles = positions[:, None] * frequency[None, :]
    cosine, sine = jnp.cos(angles), jnp.sin(angles)
    cosine = jnp.concatenate([cosine, cosine], axis=1)
    sine = jnp.concatenate([-sine, sine], axis=1)
    piece = jnp.concatenate(
        [
            jnp.concatenate([key_weight, value_weight], axis=1),
            w_query,
            w_out.T,
            jnp.zeros((1, 512), BF16),
        ],
        axis=0,
    )
    starts = jnp.concatenate([doc_start, doc_start])[None, :]
    grad_input, sums = layer(
        piece, layer_input, grad_out, starts, cosine, sine, q_gain[None, :], key_norm_gain[None, :]
    )
    fisher_value = jnp.concatenate([sums[0:ROWS], sums[ROWS : 2 * ROWS]], axis=1)
    return (fisher_value, grad_input)


def solution(mesh):
    in_specs = (
        P("seq", None),
        P("seq", None),
        P("seq"),
        P("seq", "head"),
        P("seq", "head"),
        P("seq", "head"),
        P("head", "seq"),
        P(),
        P(),
    )
    out_specs = (P("seq", "head"), P(("seq", "head"), None))
    return jax.shard_map(
        on_device, mesh=mesh, in_specs=in_specs, out_specs=out_specs, check_vma=False
    )
```

```python
import math

import jax
import jax.numpy as jnp
from jax import lax
from jax.experimental import pallas as pl
from jax.experimental.pallas import tpu as pltpu
from jax.sharding import PartitionSpec as P

HEAD_SIZE = 128
QSCALE = 168
WINDOW = 1024
NH, NZ, NY, NHEAD = 2, 16, 4, 4
SEQ = NH * NZ * NY
TOK = 128
WIDTH = 2688
ROWS = WIDTH // SEQ
SLOT = 64
FSLOT = 48
GROUP = 16
SPAN = GROUP * ROWS
WIN = 512
EDGE = 384
F32 = jnp.float32
BF16 = jnp.bfloat16


def dot(a, b, ca=1, cb=0):
    return lax.dot_general(a, b, (((ca,), (cb,)), ((), ())), preferred_element_type=F32)


def iota(shape, axis):
    return lax.broadcasted_iota(jnp.int32, shape, axis)


def rotary(normed, cosine, sine):
    return normed * cosine + pltpu.roll(normed, HEAD_SIZE // 2, 1) * sine


def norm_forward(raw, gain, cosine, sine):
    inv = lax.rsqrt(jnp.mean(raw * raw, axis=1, keepdims=True) + 1e-06)
    return rotary(raw * inv * gain, cosine, sine)


def norm_backward(grad, raw, gain, cosine, sine):
    inv = lax.rsqrt(jnp.mean(raw * raw, axis=1, keepdims=True) + 1e-06)
    back = (grad * cosine + pltpu.roll(grad * sine, HEAD_SIZE // 2, 1)) * gain
    along = jnp.mean(raw * back, axis=1, keepdims=True)
    return inv * (back - raw * (inv * inv * along))


def body(
    x_hbm, g_hbm, wk_ref, wv_ref, wq_ref, wo_ref, start_ref, cos_ref, sin_ref, qg_ref, kg_ref,
    gi_ref, fv_ref,
    x_ref, g_ref, squares, full, lhs, acc, ctx, dctx, ret, tree, treeback, qn, dqn, total, parts, arrived,
    fpad, ftwo, fsend, fy, flow, fmid, flo, flsend, usend, urecv, last, zsend, zrecv,
    kvraw,
    send_sem, recv_sem, local_sem,
):
    s = lax.axis_index("seq")
    hd = lax.axis_index("head")
    h = s // (NZ * NY)
    z = lax.rem(s // NY, NZ)
    y = lax.rem(s, NY)
    base = h * (NZ * NY)

    def at_z(step):
        return base + lax.rem(z + step + NZ, NZ) * NY + y

    def at_y(step):
        return base + z * NY + lax.rem(y + step + NY, NY)

    def shifted(step):
        return lax.rem(s + step + SEQ, SEQ)

    zi = lambda step: lax.rem(z + step + 2 * NZ, NZ)
    yi = lambda step: lax.rem(y + step + NY, NY)
    across = (1 - h) * (NZ * NY) + z * NY + y

    barrier = pltpu.get_barrier_semaphore()
    seq_partners = [at_z(1), at_z(-1), at_y(1), at_y(2), at_y(3), across]
    seq_partners += [shifted(4), shifted(-4), shifted(8), shifted(-8)]
    for partner in seq_partners:
        pl.semaphore_signal(barrier, inc=1, device_id={"seq": partner})
    for e in range(1, NHEAD):
        pl.semaphore_signal(barrier, inc=1, device_id={"head": lax.rem(hd + e, NHEAD)})
    load_x = pltpu.make_async_copy(x_hbm, x_ref, local_sem.at[0])
    load_g = pltpu.make_async_copy(g_hbm, g_ref, local_sem.at[1])
    load_x.start()
    load_g.start()

    def rows_at(first):
        return jnp.where(
            iota((SLOT, ROWS), 0) == iota((SLOT, ROWS), 1) + first, 1.0, 0.0
        ).astype(BF16)

    rest = dot(rows_at(ROWS), wq_ref[...]) + dot(rows_at(2 * ROWS), wo_ref[...], 1, 1)
    own_slot = full.at[h, z, y]
    own_slot[:, 0:256] = (dot(rows_at(0), wk_ref[...]) + rest[:, 0:256]).astype(BF16)
    own_slot[:, 256:512] = (dot(rows_at(0), wv_ref[...]) + rest[:, 256:512]).astype(BF16)
    pl.semaphore_wait(barrier, len(seq_partners) + NHEAD - 1)

    def remote(src, dst, sem, target, axis="seq"):
        return pltpu.make_async_remote_copy(
            src_ref=src,
            dst_ref=dst,
            send_sem=send_sem.at[sem],
            recv_sem=recv_sem.at[sem],
            device_id={axis: target},
        )

    def here(dst, sem):
        return remote(dst, dst, sem, across)

    HX = 0
    AZ = HX + 1
    BZ = AZ + 32
    AY = BZ + 32
    BY = AY + 96
    BX = BY + 4
    KV = BX + 16
    DK = KV + 8
    GR = DK + 16
    FY = GR + 3
    FL = FY + 6
    FH = FL + 6
    FZ = FH + 2
    HY = FZ + 15
    CY = HY + 1
    CZ = CY + 4

    side_z = lambda side: at_z(1 if side == 0 else -1)
    xs = (h, 1 - h)

    def a_piece(c, zz, yy):
        return full.at[xs[c], zz, yy, pl.ds(0, 32), :]

    def b_piece(zz, b):
        return full.at[h, zz, :, pl.ds(32 + 16 * b, 16), :]

    def az(c, k, side):
        ref = a_piece(c, zi(1 - k) if side == 0 else zi(k - 1), y)
        return remote(ref, ref, AZ + 16 * c + 2 * (k - 1) + side, side_z(side))

    def az_in(c, k, side):
        ref = a_piece(c, zi(-k) if side == 0 else zi(k), y)
        return here(ref, AZ + 16 * c + 2 * (k - 1) + side)

    def bz(b, k, side):
        ref = b_piece(zi(1 - k) if side == 0 else zi(k - 1), b)
        return remote(ref, ref, BZ + 16 * b + 2 * (k - 1) + side, side_z(side))

    def bz_in(b, k, side):
        ref = b_piece(zi(-k) if side == 0 else zi(k), b)
        return here(ref, BZ + 16 * b + 2 * (k - 1) + side)

    def bx(step, index):
        ref = full.at[h, zi(step), :, pl.ds(32, 32), pl.ds(0, EDGE)]
        return remote(ref, ref, BX + index, across)

    def bx_in(step, index):
        return here(full.at[1 - h, zi(step), :, pl.ds(32, 32), pl.ds(0, EDGE)], BX + index)

    def c_piece(zz):
        return full.at[1 - h, zz, :, pl.ds(32, 32), pl.ds(EDGE, 512 - EDGE)]

    def cz(k, side):
        ref = c_piece(zi(1 - k) if side == 0 else zi(k - 1))
        return remote(ref, ref, CZ + 2 * (k - 1) + side, side_z(side))

    def cz_in(k, side):
        return here(c_piece(zi(-k) if side == 0 else zi(k)), CZ + 2 * (k - 1) + side)

    left, right, far = yi(3), yi(1), yi(2)

    def ay_start(c, step, index):
        sem = AY + 48 * c + 3 * index
        own = a_piece(c, zi(step), y)
        remote(own, own, sem, at_y(1)).start()
        remote(own, own, sem + 1, at_y(3)).start()

    def ay_forward(c, step, index):
        sem = AY + 48 * c + 3 * index
        zz = zi(step)
        here(a_piece(c, zz, left), sem).wait_recv()
        here(a_piece(c, zz, right), sem + 1).wait_recv()
        ref = a_piece(c, zz, right if c else left)
        remote(ref, ref, sem + 2, at_y(3 if c else 1)).start()

    def ay_finish(c, step, index):
        sem = AY + 48 * c + 3 * index
        zz = zi(step)
        here(a_piece(c, zz, far), sem + 2).wait_recv()
        own = a_piece(c, zz, y)
        for i in range(3):
            here(own, sem + i).wait_send()

    def hx_piece(hh, lo, first):
        return full.at[hh, z, y, pl.ds(lo, 32), pl.ds(first, 512 - first)]

    cross = [
        remote(hx_piece(h, lo, first), hx_piece(h, lo, first), sem, across)
        for lo, first, sem in ((0, 0, HX), (32, EDGE, HY))
    ]
    for copy in cross:
        copy.start()

    def by_piece(yy, lo, n):
        return full.at[h, z, yy, pl.ds(lo, n), :]

    mine = by_piece(y, 32, 32)
    by_first = [remote(mine, mine, BY, at_y(1)), remote(mine, mine, BY + 1, at_y(3))]
    for copy in by_first:
        copy.start()
    for side in range(2):
        az(0, 1, side).start()
    ay_start(0, 0, 0)
    here(a_piece(1, z, y), HX).wait_recv()
    for side in range(2):
        az(1, 1, side).start()
    ay_start(1, 0, 0)
    here(hx_piece(1 - h, 32, EDGE), HY).wait_recv()

    def cy_piece(yy, lo, n):
        return full.at[1 - h, z, yy, pl.ds(lo, n), pl.ds(EDGE, 512 - EDGE)]

    mine = cy_piece(y, 32, 32)
    cy_first = [remote(mine, mine, CY, at_y(1)), remote(mine, mine, CY + 1, at_y(3))]
    for copy in cy_first:
        copy.start()
    up, down = by_piece(left, 32, 16), by_piece(right, 48, 16)
    by_second = [remote(up, up, BY + 2, at_y(1)), remote(down, down, BY + 3, at_y(3))]
    here(by_piece(left, 32, 32), BY).wait_recv()
    by_second[0].start()
    here(by_piece(right, 32, 32), BY + 1).wait_recv()
    by_second[1].start()
    for i in range(2):
        here(by_piece(far, 32 + 16 * i, 16), BY + 2 + i).wait_recv()
        for side in range(2):
            bz(i, 1, side).start()
    bx(0, 0).start()
    up, down = cy_piece(left, 32, 16), cy_piece(right, 48, 16)
    cy_second = [remote(up, up, CY + 2, at_y(1)), remote(down, down, CY + 3, at_y(3))]
    here(cy_piece(left, 32, 32), CY).wait_recv()
    cy_second[0].start()
    here(cy_piece(right, 32, 32), CY + 1).wait_recv()
    cy_second[1].start()
    for i in range(2):
        here(cy_piece(far, 32 + 16 * i, 16), CY + 2 + i).wait_recv()
    for side in range(2):
        cz(1, side).start()
    load_x.wait()
    load_g.wait()

    def selection(j):
        first_row = SPAN * j
        low = jnp.minimum((first_row // 128) * 128, WIDTH - WIN)
        return pl.multiple_of(low, 128), first_row - low

    def prepare(j):
        low, offset = selection(j)
        column = iota((1, GROUP * SLOT), 1)
        slot = column & (SLOT - 1)
        target = jnp.where(slot < ROWS, offset + (column >> 6) * ROWS + slot, -1)
        select = jnp.where(iota((WIN, GROUP * SLOT), 0) == target, 1.0, 0.0).astype(BF16)
        spread = dot(x_ref[:, pl.ds(low, WIN)], select)
        lhs[j, 0:TOK] = spread.astype(BF16)
        lhs[j, TOK : 2 * TOK] = pltpu.roll(spread, ROWS, 1).astype(BF16)
        spread = dot(g_ref[:, pl.ds(low, WIN)], select)
        lhs[j, 2 * TOK :] = pltpu.roll(spread, 2 * ROWS, 1).astype(BF16)
        row = iota((GROUP * FSLOT, 1), 0)
        owner = (row * 1366) >> 16
        slot = row - owner * FSLOT
        slot = jnp.where(slot < ROWS, slot, slot - ROWS)
        target = jnp.where(slot < ROWS, offset + owner * ROWS + slot, -1)
        select = jnp.where(iota((GROUP * FSLOT, WIN), 1) == target, 1.0, 0.0).astype(BF16)
        block = x_ref[:, pl.ds(low, WIN)].astype(F32)
        squares[j] = dot(select, (block * block).astype(BF16), 1, 1).astype(BF16)

    def place_of(k, side):
        return (-k if side == 0 else k), 2 * k - 1 + side

    def step_of(k, final):
        for c in range(2):
            for side in range(2):
                az_in(c, k, side).wait_recv()
                if not final or side == c:
                    az(c, k + 1, side).start()
                ay_start(c, *place_of(k, side))
        for b in range(2):
            for side in range(2):
                bz_in(b, k, side).wait_recv()
                if not final or side == b:
                    bz(b, k + 1, side).start()
        for side in range(2):
            bx(*place_of(k, side)).start()
        for side in range(2):
            cz_in(k, side).wait_recv()
            if not final or side == 0:
                cz(k + 1, side).start()

    def forward_of(k):
        for c in range(2):
            for side in range(2):
                ay_forward(c, *place_of(k, side))

    prepare(0)
    step_of(1, False)
    for c in range(2):
        ay_forward(c, 0, 0)
    prepare(1)

    def steps(k, carry):
        step_of(k, False)
        forward_of(k - 1)
        prepare(k)
        return carry

    lax.fori_loop(2, 7, steps, 0)
    step_of(7, True)
    forward_of(6)
    prepare(7)
    for c in range(2):
        az_in(c, 8, c).wait_recv()
        ay_start(c, 8, 15)
    for b in range(2):
        bz_in(b, 8, b).wait_recv()
    bx(8, 15).start()
    cz_in(8, 0).wait_recv()
    forward_of(7)
    for c in range(2):
        ay_forward(c, 8, 15)

    for copy in cross + by_first + by_second + cy_first + cy_second:
        copy.wait_send()
    for c in range(2):
        ay_finish(c, 0, 0)
    bx_in(0, 0).wait_recv()
    bx(0, 0).wait_send()

    def finish(k, carry):
        for side in range(2):
            for c in range(2):
                az(c, k, side).wait_send()
                bz(c, k, side).wait_send()
                ay_finish(c, *place_of(k, side))
            bx_in(*place_of(k, side)).wait_recv()
            bx(*place_of(k, side)).wait_send()
            cz(k, side).wait_send()
        return carry

    lax.fori_loop(1, 8, finish, 0)
    for c in range(2):
        az(c, 8, c).wait_send()
        bz(c, 8, c).wait_send()
        ay_finish(c, 8, 15)
    bx_in(8, 15).wait_recv()
    bx(8, 15).wait_send()
    cz(8, 0).wait_send()

    def weights(j):
        return full[j // 4, pl.ds(4 * lax.rem(j, 4), 4)].reshape(GROUP * SLOT, 512)

    acc[...] = jnp.zeros_like(acc)

    def project(lo, hi):
        def run(j, carry):
            acc[lo:hi] += dot(lhs[j, lo:hi], weights(j))
            return carry

        lax.fori_loop(0, SEQ // GROUP, run, 0)

    project(0, TOK)
    cosine, sine = cos_ref[...], sin_ref[...]
    q_gain, k_gain = qg_ref[...], kg_ref[...]
    for i in range(2):
        cols = slice(i * 128, (i + 1) * 128)
        ctx[0, 0, :, cols] = norm_forward(acc[0:TOK, cols], k_gain, cosine, sine).astype(BF16)
    ctx[0, 1] = acc[0:TOK, 256:512].astype(BF16)

    hop4 = remote(ctx.at[0], ctx.at[4], KV, shifted(4))
    hop8 = remote(ctx.at[4], ctx.at[8], KV + 1, shifted(4))
    hop4.start()

    def side_copies(e):
        low = jnp.where(y + e < NY, 0, 4)
        one = remote(ctx.at[low], ctx.at[e], KV + 2 * e, at_y(e))
        two = remote(ctx.at[low + 4], ctx.at[e + 4], KV + 2 * e + 1, at_y(e))
        return one, two

    for e in range(1, NY):
        @pl.when(y + e < NY)
        def _():
            side_copies(e)[0].start()
    here(ctx.at[4], KV).wait_recv()
    hop8.start()
    for e in range(1, NY):
        @pl.when(y + e < NY)
        def _():
            side_copies(e)[1].start()

        @pl.when(y + e >= NY)
        def _():
            side_copies(e)[0].start()
    project(TOK, 3 * TOK)
    here(ctx.at[8], KV + 1).wait_recv()
    for e in range(1, NY):
        @pl.when(y + e >= NY)
        def _():
            side_copies(e)[1].start()
    for i in range(4):
        cols = slice(i * 128, (i + 1) * 128)
        half = slice((i % 2) * TOK, (i % 2 + 1) * TOK)
        qn[i // 2, half] = norm_forward(
            acc[TOK : 2 * TOK, cols], q_gain, cosine, sine
        ).astype(BF16)
        dqn[i // 2, half] = acc[2 * TOK :, cols].astype(BF16)
    for e in range(1, NY):
        here(ctx.at[e], KV + 2 * e).wait_recv()
        here(ctx.at[e + 4], KV + 2 * e + 1).wait_recv()
    hop4.wait_send()
    hop8.wait_send()
    for e in range(1, NY):
        one, two = side_copies(e)
        one.wait_send()
        two.wait_send()

    scale = float(QSCALE) ** (-0.5)
    reach = 9 * TOK
    place = iota((reach, 1), 0)
    key_index = s * TOK - (place & ~(TOK - 1)) + (place & (TOK - 1))
    query_index = s * TOK + (iota((1, 2 * TOK), 1) & (TOK - 1))
    visible = (
        (key_index >= start_ref[...])
        & (key_index <= query_index)
        & (query_index - key_index < WINDOW)
    )
    for i in range(2):
        cols = slice(i * 128, (i + 1) * 128)
        keys = ctx[:, 0, :, cols].reshape(reach, 128)
        values = ctx[:, 1, :, cols].reshape(reach, 128)
        queries, douts = qn[i], dqn[i]
        scores = jnp.where(visible, dot(keys, queries, 1, 1) * scale, -jnp.inf)
        expd = jnp.exp(scores - jnp.max(scores, axis=0, keepdims=True))
        probs = expd * (1.0 / jnp.sum(expd, axis=0, keepdims=True))
        dprobs = dot(values, douts, 1, 1)
        delta = jnp.sum(probs * dprobs, axis=0, keepdims=True)
        dscores = (probs * (dprobs - delta)).astype(BF16)
        dctx[:, 0, :, cols] = (dot(dscores, queries) * scale).astype(BF16).reshape(9, TOK, 128)
        dctx[:, 1, :, cols] = dot(probs.astype(BF16), douts).astype(BF16).reshape(9, TOK, 128)
        dquery = dot(dscores, keys, 0, 0) * scale
        for r in range(2):
            col = slice((2 * i + r) * 128, (2 * i + r + 1) * 128)
            kvraw[0, :, col] = norm_backward(
                dquery[r * TOK : (r + 1) * TOK], acc[TOK : 2 * TOK, col], q_gain, cosine, sine
            ).astype(BF16)

    def side_back(e, which):
        sem = DK + 6 * which + 2 * (e - 1)
        return [
            remote(dctx.at[e + 4 * i, which], ret.at[e - 1, i, which], sem + i, at_y(NY - e))
            for i in range(2)
        ]

    def tree_back(which):
        sem = DK + 12 + 2 * which
        return [
            remote(tree.at[which, i], treeback.at[which, i], sem + i, shifted(-4 * (i + 1)))
            for i in range(2)
        ]

    for which in (1, 0):
        for e in range(1, NY):
            for copy in side_back(e, which):
                copy.start()

    def gather_sums(which):
        sums = [dctx[4 * i, which].astype(F32) for i in range(3)]
        for e in range(1, NY):
            for i in range(2):
                here(ret.at[e - 1, i, which], DK + 6 * which + 2 * (e - 1) + i).wait_recv()
            same = y + e < NY
            one = ret[e - 1, 0, which].astype(F32)
            two = ret[e - 1, 1, which].astype(F32)
            sums[0] += jnp.where(same, one, 0.0)
            sums[1] += jnp.where(same, two, one)
            sums[2] += jnp.where(same, 0.0, two)
        tree[which, 0] = sums[1].astype(BF16)
        tree[which, 1] = sums[2].astype(BF16)
        for copy in tree_back(which):
            copy.start()
        return sums[0]

    def whole(which, own):
        for i in range(2):
            here(treeback.at[which, i], DK + 12 + 2 * which + i).wait_recv()
            own = own + treeback[which, i].astype(F32)
        return own

    total[...] = jnp.zeros_like(total)

    def spread_back(which, lo, hi):
        low_slot = ROWS if which == 0 else 0

        def run(j, carry):
            low, offset = selection(j)
            out = dot(kvraw[which], weights(j), 1, 1).astype(BF16)
            row = iota((GROUP * SLOT, 1), 0)
            slot = (row & (SLOT - 1)) - low_slot
            target = jnp.where(
                (slot >= 0) & (slot < ROWS), offset + (row >> 6) * ROWS + slot, -1
            )
            select = jnp.where(iota((GROUP * SLOT, WIN), 1) == target, 1.0, 0.0).astype(BF16)
            total[:, pl.ds(low, WIN)] += dot(out, select)
            return carry

        lax.fori_loop(lo, hi, run, 0)

    spread_back(0, 0, 4)
    own_dv = gather_sums(1)
    own_dk = gather_sums(0)
    dvalue = whole(1, own_dv)

    first_cols = jnp.where(iota((GROUP, FSLOT, 128), 1) < ROWS, 1.0, 0.0)
    dv_sq = (dvalue * dvalue).astype(BF16)

    def slots(j, carry):
        both = dot(squares[j], dv_sq)
        both = both.reshape(GROUP, FSLOT, 256)
        picked = jnp.where(first_cols > 0.5, both[:, :, 0:128], both[:, :, 128:256])
        fpad[j // 4, pl.ds(4 * lax.rem(j, 4), 4)] = picked.astype(BF16).reshape(4, 4, FSLOT, 128)
        return carry

    lax.fori_loop(0, SEQ // GROUP, slots, 0)

    cross_low = remote(fpad.at[1 - h, pl.ds(0, 8)], flow, FH, across)
    cross_low.start()

    def ring(pick, buf, sem):
        return [
            remote(pick(0, far), buf.at[0], sem, at_y(1)),
            remote(pick(1, far), buf.at[1], sem + 1, at_y(3)),
            remote(pick(1, right), buf.at[2], sem + 2, at_y(1)),
            remote(pick(0, left), buf.at[3], sem + 3, at_y(3)),
        ]

    def ring_next(pick_value, buf, send, sem):
        here(buf.at[0], sem).wait_recv()
        send[0] = (pick_value(0, right) + buf[0].astype(F32)).astype(BF16)
        one = remote(send.at[0], buf.at[4], sem + 4, at_y(1))
        one.start()
        here(buf.at[1], sem + 1).wait_recv()
        send[1] = (pick_value(1, left) + buf[1].astype(F32)).astype(BF16)
        two = remote(send.at[1], buf.at[5], sem + 5, at_y(3))
        two.start()
        return [one, two]

    def ring_end(pick_value, buf, sem):
        for i in range(2, 6):
            here(buf.at[i], sem + i).wait_recv()
        first = pick_value(0, y) + buf[4].astype(F32) + buf[3].astype(F32)
        second = pick_value(1, y) + buf[2].astype(F32) + buf[5].astype(F32)
        return first, second

    up_ring = ring(lambda i, yy: fpad.at[i, pl.ds(8, 8), yy], ftwo, FY)
    for copy in up_ring:
        copy.start()
    spread_back(0, 4, 8)
    up_value = lambda i, yy: fpad[i, 8:16, yy].astype(F32)
    up_ring += ring_next(up_value, ftwo, fsend, FY)

    here(flow, FH).wait_recv()
    fmid[...] = (fpad[h, 0:8].astype(F32) + flow[...].astype(F32)).astype(BF16)
    low_ring = ring(lambda i, yy: fmid.at[pl.ds(4 * i, 4), yy], flo, FL)
    for copy in low_ring:
        copy.start()

    dkey = whole(0, own_dk)
    for i in range(2):
        cols = slice(i * 128, (i + 1) * 128)
        kvraw[1, :, cols] = norm_backward(
            dkey[:, cols], acc[0:TOK, cols], k_gain, cosine, sine
        ).astype(BF16)
    kvraw[1, :, 256:512] = dvalue.astype(BF16)
    spread_back(1, 0, 2)

    fy[0], fy[1] = ring_end(up_value, ftwo, FY)
    usend[...] = fy[1 - h].astype(BF16)
    cross_up = remote(usend, urecv, FH + 1, across)
    cross_up.start()
    low_value = lambda i, yy: fmid[4 * i : 4 * i + 4, yy].astype(F32)
    low_ring += ring_next(low_value, flo, flsend, FL)

    spread_back(1, 2, 5)
    last[0:4], last[4:8] = ring_end(low_value, flo, FL)
    here(urecv, FH + 1).wait_recv()
    last[8:16] = fy[h] + urecv[...].astype(F32)
    zsend[...] = last[...].astype(BF16)

    def to_z(d):
        return remote(zsend.at[zi(d)], zrecv.at[d - 1], FZ + d - 1, at_z(d))

    for d in (8, 7, 9, 6, 10, 5, 11, 4, 12, 3, 13, 2, 14, 1, 15):
        to_z(d).start()

    spread_back(1, 5, 8)
    for i in range(NHEAD):
        parts[i] = total[i * 32 : (i + 1) * 32].astype(BF16)
    shares = []
    for e in range(1, NHEAD):
        to = lax.rem(hd + e, NHEAD)
        shares.append(remote(parts.at[to], arrived.at[e - 1], GR + e - 1, to, "head"))
        shares[-1].start()

    sums = last[z]
    for d in range(1, NZ):
        here(zrecv.at[d - 1], FZ + d - 1).wait_recv()
        sums = sums + zrecv[d - 1].astype(F32)
    sums = sums * (1.0 / (SEQ * TOK))
    fv_ref[:, 0:128] = sums[0:ROWS]
    fv_ref[:, 128:256] = pltpu.roll(sums, FSLOT - ROWS, 0)[0:ROWS]

    for e in range(1, NHEAD):
        here(arrived.at[e - 1], GR + e - 1).wait_recv()
    mine = total[pl.ds(pl.multiple_of(hd * 32, 32), 32)]
    for e in range(1, NHEAD):
        mine = mine + arrived[e - 1].astype(F32)
    gi_ref[...] = mine.astype(BF16)

    for copy in shares + up_ring + low_ring + [cross_low, cross_up]:
        copy.wait_send()
    for d in range(1, NZ):
        to_z(d).wait_send()
    for which in range(2):
        for copy in tree_back(which):
            copy.wait_send()
        for e in range(1, NY):
            for copy in side_back(e, which):
                copy.wait_send()


def layer(*operands):
    vmem = pl.BlockSpec(memory_space=pltpu.VMEM)
    sems = 320
    return pl.pallas_call(
        body,
        name="layer_backward",
        out_shape=(
            jax.ShapeDtypeStruct((32, WIDTH), BF16),
            jax.ShapeDtypeStruct((ROWS, 256), F32),
        ),
        in_specs=[pl.BlockSpec(memory_space=pl.ANY)] * 2 + [vmem] * 9,
        out_specs=(vmem, vmem),
        scratch_shapes=[
            pltpu.VMEM((TOK, WIDTH), BF16),
            pltpu.VMEM((TOK, WIDTH), BF16),
            pltpu.VMEM((SEQ // GROUP, GROUP * FSLOT, TOK), BF16),
            pltpu.VMEM((NH, NZ, NY, SLOT, 512), BF16),
            pltpu.VMEM((SEQ // GROUP, 3 * TOK, GROUP * SLOT), BF16),
            pltpu.VMEM((3 * TOK, 512), F32),
            pltpu.VMEM((9, 2, TOK, 256), BF16),
            pltpu.VMEM((9, 2, TOK, 256), BF16),
            pltpu.VMEM((3, 2, 2, TOK, 256), BF16),
            pltpu.VMEM((2, 2, TOK, 256), BF16),
            pltpu.VMEM((2, 2, TOK, 256), BF16),
            pltpu.VMEM((2, 2 * TOK, 128), BF16),
            pltpu.VMEM((2, 2 * TOK, 128), BF16),
            pltpu.VMEM((TOK, WIDTH), F32),
            pltpu.VMEM((NHEAD, 32, WIDTH), BF16),
            pltpu.VMEM((NHEAD - 1, 32, WIDTH), BF16),
            pltpu.VMEM((NH, NZ, NY, FSLOT, 128), BF16),
            pltpu.VMEM((6, 8, FSLOT, 128), BF16),
            pltpu.VMEM((2, 8, FSLOT, 128), BF16),
            pltpu.VMEM((NH, 8, FSLOT, 128), F32),
            pltpu.VMEM((8, NY, FSLOT, 128), BF16),
            pltpu.VMEM((8, NY, FSLOT, 128), BF16),
            pltpu.VMEM((6, 4, FSLOT, 128), BF16),
            pltpu.VMEM((2, 4, FSLOT, 128), BF16),
            pltpu.VMEM((8, FSLOT, 128), BF16),
            pltpu.VMEM((8, FSLOT, 128), BF16),
            pltpu.VMEM((NZ, FSLOT, 128), F32),
            pltpu.VMEM((NZ, FSLOT, 128), BF16),
            pltpu.VMEM((NZ - 1, FSLOT, 128), BF16),
            pltpu.VMEM((2, TOK, 512), BF16),
            pltpu.SemaphoreType.DMA((sems,)),
            pltpu.SemaphoreType.DMA((sems,)),
            pltpu.SemaphoreType.DMA((2,)),
        ],
        compiler_params=pltpu.CompilerParams(
            collective_id=0, has_side_effects=True, vmem_limit_bytes=60 * 1024 * 1024
        ),
    )(*operands)


def on_device(
    layer_input,
    grad_out,
    doc_start,
    w_query,
    key_weight,
    value_weight,
    w_out,
    q_gain,
    key_norm_gain,
):
    seq_index = lax.axis_index("seq")
    token_index = seq_index * TOK + jnp.arange(TOK, dtype=jnp.int32)
    positions = (token_index - doc_start).astype(F32)
    half = HEAD_SIZE // 2
    frequency = jnp.exp(jnp.arange(half).astype(F32) * (-math.log(10000.0) / half))
    angles = positions[:, None] * frequency[None, :]
    cosine, sine = jnp.cos(angles), jnp.sin(angles)
    cosine = jnp.concatenate([cosine, cosine], axis=1)
    sine = jnp.concatenate([-sine, sine], axis=1)
    starts = jnp.concatenate([doc_start, doc_start])[None, :]
    grad_input, fisher_value = layer(
        layer_input, grad_out, key_weight, value_weight, w_query, w_out, starts, cosine, sine,
        q_gain[None, :], key_norm_gain[None, :],
    )
    return (fisher_value, grad_input)


def solution(mesh):
    in_specs = (
        P("seq", None),
        P("seq", None),
        P("seq"),
        P("seq", "head"),
        P("seq", "head"),
        P("seq", "head"),
        P("head", "seq"),
        P(),
        P(),
    )
    out_specs = (P("seq", "head"), P(("seq", "head"), None))
    return jax.shard_map(
        on_device, mesh=mesh, in_specs=in_specs, out_specs=out_specs, check_vma=False
    )
```

```python
import math

import jax
import jax.numpy as jnp
from jax import lax
from jax.experimental import pallas as pl
from jax.experimental.pallas import tpu as pltpu
from jax.sharding import PartitionSpec as P

HEAD_SIZE = 128
QSCALE = 168
WINDOW = 1024
NH, NZ, NY, NHEAD = 2, 16, 4, 4
SEQ = NH * NZ * NY
TOK = 128
WIDTH = 2688
ROWS = WIDTH // SEQ
SLOT = 64
FSLOT = 48
GROUP = 16
SPAN = GROUP * ROWS
WIN = 512
EDGE = 384
F32 = jnp.float32
BF16 = jnp.bfloat16


def dot(a, b, ca=1, cb=0):
    return lax.dot_general(a, b, (((ca,), (cb,)), ((), ())), preferred_element_type=F32)


def iota(shape, axis):
    return lax.broadcasted_iota(jnp.int32, shape, axis)


def rotary(normed, cosine, sine):
    return normed * cosine + pltpu.roll(normed, HEAD_SIZE // 2, 1) * sine


def norm_forward(raw, gain, cosine, sine):
    inv = lax.rsqrt(jnp.mean(raw * raw, axis=1, keepdims=True) + 1e-06)
    return rotary(raw * inv * gain, cosine, sine)


def norm_backward(grad, raw, gain, cosine, sine):
    inv = lax.rsqrt(jnp.mean(raw * raw, axis=1, keepdims=True) + 1e-06)
    back = (grad * cosine + pltpu.roll(grad * sine, HEAD_SIZE // 2, 1)) * gain
    along = jnp.mean(raw * back, axis=1, keepdims=True)
    return inv * (back - raw * (inv * inv * along))


def body(
    x_hbm, g_hbm, wk_ref, wv_ref, wq_ref, wo_ref, start_ref, cos_ref, sin_ref, qg_ref, kg_ref,
    gi_ref, fv_ref,
    x_ref, g_ref, squares, full, lhs, acc, ctx, dctx, ret, tree, treeback, qn, dqn, total, parts, arrived,
    fpad, ftwo, fsend, fy, flow, fmid, flo, flsend, usend, urecv, last, zsend, zrecv,
    kvraw,
    send_sem, recv_sem, local_sem,
):
    s = lax.axis_index("seq")
    hd = lax.axis_index("head")
    h = s // (NZ * NY)
    z = lax.rem(s // NY, NZ)
    y = lax.rem(s, NY)
    base = h * (NZ * NY)

    def at_z(step):
        return base + lax.rem(z + step + NZ, NZ) * NY + y

    def at_y(step):
        return base + z * NY + lax.rem(y + step + NY, NY)

    def shifted(step):
        return lax.rem(s + step + SEQ, SEQ)

    zi = lambda step: lax.rem(z + step + 2 * NZ, NZ)
    yi = lambda step: lax.rem(y + step + NY, NY)
    across = (1 - h) * (NZ * NY) + z * NY + y

    barrier = pltpu.get_barrier_semaphore()
    seq_partners = [at_z(1), at_z(-1), at_y(1), at_y(2), at_y(3), across]
    seq_partners += [shifted(4), shifted(-4), shifted(8), shifted(-8)]
    for partner in seq_partners:
        pl.semaphore_signal(barrier, inc=1, device_id={"seq": partner})
    for e in range(1, NHEAD):
        pl.semaphore_signal(barrier, inc=1, device_id={"head": lax.rem(hd + e, NHEAD)})
    load_x = pltpu.make_async_copy(x_hbm, x_ref, local_sem.at[0])
    load_g = pltpu.make_async_copy(g_hbm, g_ref, local_sem.at[1])
    load_x.start()
    load_g.start()

    def rows_at(first):
        return jnp.where(
            iota((SLOT, ROWS), 0) == iota((SLOT, ROWS), 1) + first, 1.0, 0.0
        ).astype(BF16)

    rest = dot(rows_at(ROWS), wq_ref[...]) + dot(rows_at(2 * ROWS), wo_ref[...])
    own_slot = full.at[h, z, y]
    own_slot[:, 0:256] = (dot(rows_at(0), wk_ref[...]) + rest[:, 0:256]).astype(BF16)
    own_slot[:, 256:512] = (dot(rows_at(0), wv_ref[...]) + rest[:, 256:512]).astype(BF16)
    pl.semaphore_wait(barrier, len(seq_partners) + NHEAD - 1)

    def remote(src, dst, sem, target, axis="seq"):
        return pltpu.make_async_remote_copy(
            src_ref=src,
            dst_ref=dst,
            send_sem=send_sem.at[sem],
            recv_sem=recv_sem.at[sem],
            device_id={axis: target},
        )

    def here(dst, sem):
        return remote(dst, dst, sem, across)

    HX = 0
    AZ = HX + 1
    BZ = AZ + 32
    AY = BZ + 32
    BY = AY + 96
    BX = BY + 4
    KV = BX + 16
    DK = KV + 8
    GR = DK + 16
    FY = GR + 3
    FL = FY + 6
    FH = FL + 6
    FZ = FH + 2
    HY = FZ + 15
    CY = HY + 1
    CZ = CY + 4

    side_z = lambda side: at_z(1 if side == 0 else -1)
    xs = (h, 1 - h)

    def a_piece(c, zz, yy):
        return full.at[xs[c], zz, yy, pl.ds(0, 32), :]

    def b_piece(zz, b):
        return full.at[h, zz, :, pl.ds(32 + 16 * b, 16), :]

    def az(c, k, side):
        ref = a_piece(c, zi(1 - k) if side == 0 else zi(k - 1), y)
        return remote(ref, ref, AZ + 16 * c + 2 * (k - 1) + side, side_z(side))

    def az_in(c, k, side):
        ref = a_piece(c, zi(-k) if side == 0 else zi(k), y)
        return here(ref, AZ + 16 * c + 2 * (k - 1) + side)

    def bz(b, k, side):
        ref = b_piece(zi(1 - k) if side == 0 else zi(k - 1), b)
        return remote(ref, ref, BZ + 16 * b + 2 * (k - 1) + side, side_z(side))

    def bz_in(b, k, side):
        ref = b_piece(zi(-k) if side == 0 else zi(k), b)
        return here(ref, BZ + 16 * b + 2 * (k - 1) + side)

    def bx(step, index):
        ref = full.at[h, zi(step), :, pl.ds(32, 32), pl.ds(0, EDGE)]
        return remote(ref, ref, BX + index, across)

    def bx_in(step, index):
        return here(full.at[1 - h, zi(step), :, pl.ds(32, 32), pl.ds(0, EDGE)], BX + index)

    def c_piece(zz):
        return full.at[1 - h, zz, :, pl.ds(32, 32), pl.ds(EDGE, 512 - EDGE)]

    def cz(k, side):
        ref = c_piece(zi(1 - k) if side == 0 else zi(k - 1))
        return remote(ref, ref, CZ + 2 * (k - 1) + side, side_z(side))

    def cz_in(k, side):
        return here(c_piece(zi(-k) if side == 0 else zi(k)), CZ + 2 * (k - 1) + side)

    left, right, far = yi(3), yi(1), yi(2)

    def ay_start(c, step, index):
        sem = AY + 48 * c + 3 * index
        own = a_piece(c, zi(step), y)
        remote(own, own, sem, at_y(1)).start()
        remote(own, own, sem + 1, at_y(3)).start()

    def ay_forward(c, step, index):
        sem = AY + 48 * c + 3 * index
        zz = zi(step)
        here(a_piece(c, zz, left), sem).wait_recv()
        here(a_piece(c, zz, right), sem + 1).wait_recv()
        ref = a_piece(c, zz, right if c else left)
        remote(ref, ref, sem + 2, at_y(3 if c else 1)).start()

    def ay_finish(c, step, index):
        sem = AY + 48 * c + 3 * index
        zz = zi(step)
        here(a_piece(c, zz, far), sem + 2).wait_recv()
        own = a_piece(c, zz, y)
        for i in range(3):
            here(own, sem + i).wait_send()

    def place_of(k, side):
        return (-k if side == 0 else k), 2 * k - 1 + side

    def first_step(k, final=False):
        for c in range(2):
            for side in range(2):
                az_in(c, k, side).wait_recv()
                if not final or side == c:
                    az(c, k + 1, side).start()
                ay_start(c, *place_of(k, side))

    def hx_piece(hh, lo, first):
        return full.at[hh, z, y, pl.ds(lo, 32), pl.ds(first, 512 - first)]

    cross = [
        remote(hx_piece(h, lo, first), hx_piece(h, lo, first), sem, across)
        for lo, first, sem in ((0, 0, HX), (32, EDGE, HY))
    ]
    for copy in cross:
        copy.start()

    def by_piece(yy, lo, n):
        return full.at[h, z, yy, pl.ds(lo, n), :]

    mine = by_piece(y, 32, 32)
    by_first = [remote(mine, mine, BY, at_y(1)), remote(mine, mine, BY + 1, at_y(3))]
    for copy in by_first:
        copy.start()
    for side in range(2):
        az(0, 1, side).start()
    ay_start(0, 0, 0)
    here(a_piece(1, z, y), HX).wait_recv()
    for side in range(2):
        az(1, 1, side).start()
    ay_start(1, 0, 0)
    here(hx_piece(1 - h, 32, EDGE), HY).wait_recv()

    def cy_piece(yy, lo, n):
        return full.at[1 - h, z, yy, pl.ds(lo, n), pl.ds(EDGE, 512 - EDGE)]

    mine = cy_piece(y, 32, 32)
    cy_first = [remote(mine, mine, CY, at_y(1)), remote(mine, mine, CY + 1, at_y(3))]
    for copy in cy_first:
        copy.start()
    up, down = by_piece(left, 32, 16), by_piece(right, 48, 16)
    by_second = [remote(up, up, BY + 2, at_y(1)), remote(down, down, BY + 3, at_y(3))]
    here(by_piece(left, 32, 32), BY).wait_recv()
    by_second[0].start()
    here(by_piece(right, 32, 32), BY + 1).wait_recv()
    by_second[1].start()
    first_step(1)
    for i in range(2):
        here(by_piece(far, 32 + 16 * i, 16), BY + 2 + i).wait_recv()
        for side in range(2):
            bz(i, 1, side).start()
    bx(0, 0).start()
    up, down = cy_piece(left, 32, 16), cy_piece(right, 48, 16)
    cy_second = [remote(up, up, CY + 2, at_y(1)), remote(down, down, CY + 3, at_y(3))]
    here(cy_piece(left, 32, 32), CY).wait_recv()
    cy_second[0].start()
    here(cy_piece(right, 32, 32), CY + 1).wait_recv()
    cy_second[1].start()
    first_step(2)
    for i in range(2):
        here(cy_piece(far, 32 + 16 * i, 16), CY + 2 + i).wait_recv()
    for side in range(2):
        cz(1, side).start()

    def selection(j):
        first_row = SPAN * j
        low = jnp.minimum((first_row // 128) * 128, WIDTH - WIN)
        return pl.multiple_of(low, 128), first_row - low

    def prepare(j):
        low, offset = selection(j)
        column = iota((1, GROUP * SLOT), 1)
        slot = column & (SLOT - 1)
        target = jnp.where(slot < ROWS, offset + (column >> 6) * ROWS + slot, -1)
        select = jnp.where(iota((WIN, GROUP * SLOT), 0) == target, 1.0, 0.0).astype(BF16)
        spread = dot(x_ref[:, pl.ds(low, WIN)], select)
        lhs[j, 0:TOK] = spread.astype(BF16)
        lhs[j, TOK : 2 * TOK] = pltpu.roll(spread, ROWS, 1).astype(BF16)
        spread = dot(g_ref[:, pl.ds(low, WIN)], select)
        lhs[j, 2 * TOK :] = pltpu.roll(spread, 2 * ROWS, 1).astype(BF16)
        row = iota((GROUP * FSLOT, 1), 0)
        owner = (row * 1366) >> 16
        slot = row - owner * FSLOT
        slot = jnp.where(slot < ROWS, slot, slot - ROWS)
        target = jnp.where(slot < ROWS, offset + owner * ROWS + slot, -1)
        select = jnp.where(iota((GROUP * FSLOT, WIN), 1) == target, 1.0, 0.0).astype(BF16)
        block = x_ref[:, pl.ds(low, WIN)].astype(F32)
        squares[j] = dot(select, (block * block).astype(BF16), 1, 1).astype(BF16)

    def step_of(k, final=False):
        for b in range(2):
            for side in range(2):
                bz_in(b, k, side).wait_recv()
                if not final or side == b:
                    bz(b, k + 1, side).start()
        for side in range(2):
            bx(*place_of(k, side)).start()
        for side in range(2):
            cz_in(k, side).wait_recv()
            if not final or side == 0:
                cz(k + 1, side).start()

    def forward_of(k):
        for c in range(2):
            for side in range(2):
                ay_forward(c, *place_of(k, side))

    load_x.wait()
    load_g.wait()
    prepare(0)
    step_of(1)
    first_step(3)
    for c in range(2):
        ay_forward(c, 0, 0)
    forward_of(1)

    def steps(k, carry):
        step_of(k)
        first_step(k + 2)
        forward_of(k)
        prepare(k - 1)
        return carry

    lax.fori_loop(2, 5, steps, 0)
    step_of(5)
    first_step(7, True)
    forward_of(5)
    prepare(4)
    step_of(6)
    for c in range(2):
        az_in(c, 8, c).wait_recv()
        ay_start(c, 8, 15)
    forward_of(6)
    prepare(5)
    step_of(7, True)
    forward_of(7)
    prepare(6)
    for c in range(2):
        ay_forward(c, 8, 15)
    for b in range(2):
        bz_in(b, 8, b).wait_recv()
    bx(8, 15).start()
    cz_in(8, 0).wait_recv()
    prepare(7)

    for copy in cross + by_first + by_second + cy_first + cy_second:
        copy.wait_send()
    for c in range(2):
        ay_finish(c, 0, 0)
    bx_in(0, 0).wait_recv()
    bx(0, 0).wait_send()

    def finish(k, carry):
        for side in range(2):
            for c in range(2):
                az(c, k, side).wait_send()
                bz(c, k, side).wait_send()
                ay_finish(c, *place_of(k, side))
            bx_in(*place_of(k, side)).wait_recv()
            bx(*place_of(k, side)).wait_send()
            cz(k, side).wait_send()
        return carry

    lax.fori_loop(1, 8, finish, 0)
    for c in range(2):
        az(c, 8, c).wait_send()
        bz(c, 8, c).wait_send()
        ay_finish(c, 8, 15)
    bx_in(8, 15).wait_recv()
    bx(8, 15).wait_send()
    cz(8, 0).wait_send()

    def weights(j):
        return full[j // 4, pl.ds(4 * lax.rem(j, 4), 4)].reshape(GROUP * SLOT, 512)

    acc[...] = jnp.zeros_like(acc)

    def project(lo, hi):
        def run(j, carry):
            acc[lo:hi] += dot(lhs[j, lo:hi], weights(j))
            return carry

        lax.fori_loop(0, SEQ // GROUP, run, 0)

    project(0, TOK)
    cosine = jnp.concatenate([cos_ref[...], cos_ref[...]], axis=1)
    sine = jnp.concatenate([-sin_ref[...], sin_ref[...]], axis=1)
    q_gain, k_gain = qg_ref[...], kg_ref[...]
    for i in range(2):
        cols = slice(i * 128, (i + 1) * 128)
        ctx[0, 0, :, cols] = norm_forward(acc[0:TOK, cols], k_gain, cosine, sine).astype(BF16)
    ctx[0, 1] = acc[0:TOK, 256:512].astype(BF16)

    hop4 = remote(ctx.at[0], ctx.at[4], KV, shifted(4))
    hop8 = remote(ctx.at[4], ctx.at[8], KV + 1, shifted(4))
    hop4.start()

    def side_copies(e):
        low = jnp.where(y + e < NY, 0, 4)
        one = remote(ctx.at[low], ctx.at[e], KV + 2 * e, at_y(e))
        two = remote(ctx.at[low + 4], ctx.at[e + 4], KV + 2 * e + 1, at_y(e))
        return one, two

    for e in range(1, NY):
        @pl.when(y + e < NY)
        def _():
            side_copies(e)[0].start()
    here(ctx.at[4], KV).wait_recv()
    hop8.start()
    for e in range(1, NY):
        @pl.when(y + e < NY)
        def _():
            side_copies(e)[1].start()

        @pl.when(y + e >= NY)
        def _():
            side_copies(e)[0].start()
    project(TOK, 3 * TOK)
    here(ctx.at[8], KV + 1).wait_recv()
    for e in range(1, NY):
        @pl.when(y + e >= NY)
        def _():
            side_copies(e)[1].start()
    for i in range(4):
        cols = slice(i * 128, (i + 1) * 128)
        half = slice((i % 2) * TOK, (i % 2 + 1) * TOK)
        qn[i // 2, half] = norm_forward(
            acc[TOK : 2 * TOK, cols], q_gain, cosine, sine
        ).astype(BF16)
        dqn[i // 2, half] = acc[2 * TOK :, cols].astype(BF16)
    for e in range(1, NY):
        here(ctx.at[e], KV + 2 * e).wait_recv()
        here(ctx.at[e + 4], KV + 2 * e + 1).wait_recv()
    hop4.wait_send()
    hop8.wait_send()
    for e in range(1, NY):
        one, two = side_copies(e)
        one.wait_send()
        two.wait_send()

    scale = float(QSCALE) ** (-0.5)
    reach = 9 * TOK
    place = iota((reach, 1), 0)
    key_index = s * TOK - (place & ~(TOK - 1)) + (place & (TOK - 1))
    query_index = s * TOK + (iota((1, 2 * TOK), 1) & (TOK - 1))
    visible = (
        (key_index >= jnp.concatenate([start_ref[...], start_ref[...]], axis=1))
        & (key_index <= query_index)
        & (query_index - key_index < WINDOW)
    )
    for i in range(2):
        cols = slice(i * 128, (i + 1) * 128)
        keys = ctx[:, 0, :, cols].reshape(reach, 128)
        values = ctx[:, 1, :, cols].reshape(reach, 128)
        queries, douts = qn[i], dqn[i]
        scores = jnp.where(visible, dot(keys, queries, 1, 1) * scale, -jnp.inf)
        expd = jnp.exp(scores - jnp.max(scores, axis=0, keepdims=True))
        probs = expd * (1.0 / jnp.sum(expd, axis=0, keepdims=True))
        dprobs = dot(values, douts, 1, 1)
        delta = jnp.sum(probs * dprobs, axis=0, keepdims=True)
        dscores = (probs * (dprobs - delta)).astype(BF16)
        dctx[:, 0, :, cols] = (dot(dscores, queries) * scale).astype(BF16).reshape(9, TOK, 128)
        dctx[:, 1, :, cols] = dot(probs.astype(BF16), douts).astype(BF16).reshape(9, TOK, 128)
        dquery = dot(dscores, keys, 0, 0) * scale
        for r in range(2):
            col = slice((2 * i + r) * 128, (2 * i + r + 1) * 128)
            kvraw[0, :, col] = norm_backward(
                dquery[r * TOK : (r + 1) * TOK], acc[TOK : 2 * TOK, col], q_gain, cosine, sine
            ).astype(BF16)

    def side_back(e, which):
        sem = DK + 6 * which + 2 * (e - 1)
        return [
            remote(dctx.at[e + 4 * i, which], ret.at[e - 1, i, which], sem + i, at_y(NY - e))
            for i in range(2)
        ]

    def tree_back(which):
        sem = DK + 12 + 2 * which
        return [
            remote(tree.at[which, i], treeback.at[which, i], sem + i, shifted(-4 * (i + 1)))
            for i in range(2)
        ]

    for which in (1, 0):
        for e in range(1, NY):
            for copy in side_back(e, which):
                copy.start()

    def gather_sums(which):
        sums = [dctx[4 * i, which].astype(F32) for i in range(3)]
        for e in range(1, NY):
            for i in range(2):
                here(ret.at[e - 1, i, which], DK + 6 * which + 2 * (e - 1) + i).wait_recv()
            same = y + e < NY
            one = ret[e - 1, 0, which].astype(F32)
            two = ret[e - 1, 1, which].astype(F32)
            sums[0] += jnp.where(same, one, 0.0)
            sums[1] += jnp.where(same, two, one)
            sums[2] += jnp.where(same, 0.0, two)
        tree[which, 0] = sums[1].astype(BF16)
        tree[which, 1] = sums[2].astype(BF16)
        for copy in tree_back(which):
            copy.start()
        return sums[0]

    def whole(which, own):
        for i in range(2):
            here(treeback.at[which, i], DK + 12 + 2 * which + i).wait_recv()
            own = own + treeback[which, i].astype(F32)
        return own

    total[...] = jnp.zeros_like(total)

    def spread_back(which, lo, hi):
        low_slot = ROWS if which == 0 else 0

        def run(j, carry):
            low, offset = selection(j)
            out = dot(kvraw[which], weights(j), 1, 1).astype(BF16)
            row = iota((GROUP * SLOT, 1), 0)
            slot = (row & (SLOT - 1)) - low_slot
            target = jnp.where(
                (slot >= 0) & (slot < ROWS), offset + (row >> 6) * ROWS + slot, -1
            )
            select = jnp.where(iota((GROUP * SLOT, WIN), 1) == target, 1.0, 0.0).astype(BF16)
            total[:, pl.ds(low, WIN)] += dot(out, select)
            return carry

        lax.fori_loop(lo, hi, run, 0)

    spread_back(0, 0, 4)
    own_dv = gather_sums(1)
    own_dk = gather_sums(0)
    dvalue = whole(1, own_dv)

    first_cols = jnp.where(iota((GROUP, FSLOT, 128), 1) < ROWS, 1.0, 0.0)
    dv_sq = (dvalue * dvalue).astype(BF16)

    def slots(j, carry):
        both = dot(squares[j], dv_sq)
        both = both.reshape(GROUP, FSLOT, 256)
        picked = jnp.where(first_cols > 0.5, both[:, :, 0:128], both[:, :, 128:256])
        fpad[j // 4, pl.ds(4 * lax.rem(j, 4), 4)] = picked.astype(BF16).reshape(4, 4, FSLOT, 128)
        return carry

    lax.fori_loop(0, SEQ // GROUP, slots, 0)

    cross_low = remote(fpad.at[1 - h, pl.ds(0, 8)], flow, FH, across)
    cross_low.start()

    def ring(pick, buf, sem):
        return [
            remote(pick(0, far), buf.at[0], sem, at_y(1)),
            remote(pick(1, far), buf.at[1], sem + 1, at_y(3)),
            remote(pick(1, right), buf.at[2], sem + 2, at_y(1)),
            remote(pick(0, left), buf.at[3], sem + 3, at_y(3)),
        ]

    def ring_next(pick_value, buf, send, sem):
        here(buf.at[0], sem).wait_recv()
        send[0] = (pick_value(0, right) + buf[0].astype(F32)).astype(BF16)
        one = remote(send.at[0], buf.at[4], sem + 4, at_y(1))
        one.start()
        here(buf.at[1], sem + 1).wait_recv()
        send[1] = (pick_value(1, left) + buf[1].astype(F32)).astype(BF16)
        two = remote(send.at[1], buf.at[5], sem + 5, at_y(3))
        two.start()
        return [one, two]

    def ring_end(pick_value, buf, sem):
        for i in range(2, 6):
            here(buf.at[i], sem + i).wait_recv()
        first = pick_value(0, y) + buf[4].astype(F32) + buf[3].astype(F32)
        second = pick_value(1, y) + buf[2].astype(F32) + buf[5].astype(F32)
        return first, second

    up_ring = ring(lambda i, yy: fpad.at[i, pl.ds(8, 8), yy], ftwo, FY)
    for copy in up_ring:
        copy.start()
    spread_back(0, 4, 8)
    up_value = lambda i, yy: fpad[i, 8:16, yy].astype(F32)
    up_ring += ring_next(up_value, ftwo, fsend, FY)

    here(flow, FH).wait_recv()
    fmid[...] = (fpad[h, 0:8].astype(F32) + flow[...].astype(F32)).astype(BF16)
    low_ring = ring(lambda i, yy: fmid.at[pl.ds(4 * i, 4), yy], flo, FL)
    for copy in low_ring:
        copy.start()

    dkey = whole(0, own_dk)
    for i in range(2):
        cols = slice(i * 128, (i + 1) * 128)
        kvraw[1, :, cols] = norm_backward(
            dkey[:, cols], acc[0:TOK, cols], k_gain, cosine, sine
        ).astype(BF16)
    kvraw[1, :, 256:512] = dvalue.astype(BF16)
    spread_back(1, 0, 2)

    fy[0], fy[1] = ring_end(up_value, ftwo, FY)
    usend[...] = fy[1 - h].astype(BF16)
    cross_up = remote(usend, urecv, FH + 1, across)
    cross_up.start()
    low_value = lambda i, yy: fmid[4 * i : 4 * i + 4, yy].astype(F32)
    low_ring += ring_next(low_value, flo, flsend, FL)

    spread_back(1, 2, 5)
    last[0:4], last[4:8] = ring_end(low_value, flo, FL)
    here(urecv, FH + 1).wait_recv()
    last[8:16] = fy[h] + urecv[...].astype(F32)
    zsend[...] = last[...].astype(BF16)

    def to_z(d):
        return remote(zsend.at[zi(d)], zrecv.at[d - 1], FZ + d - 1, at_z(d))

    for d in (8, 7, 9, 6, 10, 5, 11, 4, 12, 3, 13, 2, 14, 1, 15):
        to_z(d).start()

    spread_back(1, 5, 8)
    for i in range(NHEAD):
        parts[i] = total[i * 32 : (i + 1) * 32].astype(BF16)
    shares = []
    for e in range(1, NHEAD):
        to = lax.rem(hd + e, NHEAD)
        shares.append(remote(parts.at[to], arrived.at[e - 1], GR + e - 1, to, "head"))
        shares[-1].start()

    sums = last[z]
    for d in range(1, NZ):
        here(zrecv.at[d - 1], FZ + d - 1).wait_recv()
        sums = sums + zrecv[d - 1].astype(F32)
    sums = sums * (1.0 / (SEQ * TOK))
    fv_ref[:, 0:128] = sums[0:ROWS]
    fv_ref[:, 128:256] = pltpu.roll(sums, FSLOT - ROWS, 0)[0:ROWS]

    for e in range(1, NHEAD):
        here(arrived.at[e - 1], GR + e - 1).wait_recv()
    mine = total[pl.ds(pl.multiple_of(hd * 32, 32), 32)]
    for e in range(1, NHEAD):
        mine = mine + arrived[e - 1].astype(F32)
    gi_ref[...] = mine.astype(BF16)

    for copy in shares + up_ring + low_ring + [cross_low, cross_up]:
        copy.wait_send()
    for d in range(1, NZ):
        to_z(d).wait_send()
    for which in range(2):
        for copy in tree_back(which):
            copy.wait_send()
        for e in range(1, NY):
            for copy in side_back(e, which):
                copy.wait_send()


def layer(*operands):
    vmem = pl.BlockSpec(memory_space=pltpu.VMEM)
    sems = 320
    return pl.pallas_call(
        body,
        name="layer_backward",
        out_shape=(
            jax.ShapeDtypeStruct((32, WIDTH), BF16),
            jax.ShapeDtypeStruct((ROWS, 256), F32),
        ),
        in_specs=[pl.BlockSpec(memory_space=pl.ANY)] * 2 + [vmem] * 9,
        out_specs=(vmem, vmem),
        scratch_shapes=[
            pltpu.VMEM((TOK, WIDTH), BF16),
            pltpu.VMEM((TOK, WIDTH), BF16),
            pltpu.VMEM((SEQ // GROUP, GROUP * FSLOT, TOK), BF16),
            pltpu.VMEM((NH, NZ, NY, SLOT, 512), BF16),
            pltpu.VMEM((SEQ // GROUP, 3 * TOK, GROUP * SLOT), BF16),
            pltpu.VMEM((3 * TOK, 512), F32),
            pltpu.VMEM((9, 2, TOK, 256), BF16),
            pltpu.VMEM((9, 2, TOK, 256), BF16),
            pltpu.VMEM((3, 2, 2, TOK, 256), BF16),
            pltpu.VMEM((2, 2, TOK, 256), BF16),
            pltpu.VMEM((2, 2, TOK, 256), BF16),
            pltpu.VMEM((2, 2 * TOK, 128), BF16),
            pltpu.VMEM((2, 2 * TOK, 128), BF16),
            pltpu.VMEM((TOK, WIDTH), F32),
            pltpu.VMEM((NHEAD, 32, WIDTH), BF16),
            pltpu.VMEM((NHEAD - 1, 32, WIDTH), BF16),
            pltpu.VMEM((NH, NZ, NY, FSLOT, 128), BF16),
            pltpu.VMEM((6, 8, FSLOT, 128), BF16),
            pltpu.VMEM((2, 8, FSLOT, 128), BF16),
            pltpu.VMEM((NH, 8, FSLOT, 128), F32),
            pltpu.VMEM((8, NY, FSLOT, 128), BF16),
            pltpu.VMEM((8, NY, FSLOT, 128), BF16),
            pltpu.VMEM((6, 4, FSLOT, 128), BF16),
            pltpu.VMEM((2, 4, FSLOT, 128), BF16),
            pltpu.VMEM((8, FSLOT, 128), BF16),
            pltpu.VMEM((8, FSLOT, 128), BF16),
            pltpu.VMEM((NZ, FSLOT, 128), F32),
            pltpu.VMEM((NZ, FSLOT, 128), BF16),
            pltpu.VMEM((NZ - 1, FSLOT, 128), BF16),
            pltpu.VMEM((2, TOK, 512), BF16),
            pltpu.SemaphoreType.DMA((sems,)),
            pltpu.SemaphoreType.DMA((sems,)),
            pltpu.SemaphoreType.DMA((2,)),
        ],
        compiler_params=pltpu.CompilerParams(
            collective_id=0, has_side_effects=True, vmem_limit_bytes=60 * 1024 * 1024
        ),
    )(*operands)


def on_device(
    layer_input,
    grad_out,
    doc_start,
    w_query,
    key_weight,
    value_weight,
    w_out,
    q_gain,
    key_norm_gain,
):
    seq_index = lax.axis_index("seq")
    token_index = seq_index * TOK + jnp.arange(TOK, dtype=jnp.int32)
    positions = (token_index - doc_start).astype(F32)
    half = HEAD_SIZE // 2
    frequency = jnp.exp(jnp.arange(half).astype(F32) * (-math.log(10000.0) / half))
    angles = positions[:, None] * frequency[None, :]
    cosine, sine = jnp.cos(angles), jnp.sin(angles)
    grad_input, fisher_value = layer(
        layer_input, grad_out, key_weight, value_weight, w_query, w_out.T, doc_start[None, :],
        cosine, sine,
        q_gain[None, :], key_norm_gain[None, :],
    )
    return (fisher_value, grad_input)


def solution(mesh):
    in_specs = (
        P("seq", None),
        P("seq", None),
        P("seq"),
        P("seq", "head"),
        P("seq", "head"),
        P("seq", "head"),
        P("head", "seq"),
        P(),
        P(),
    )
    out_specs = (P("seq", "head"), P(("seq", "head"), None))
    return jax.shard_map(
        on_device, mesh=mesh, in_specs=in_specs, out_specs=out_specs, check_vma=False
    )
```

```python
import math

import jax
import jax.numpy as jnp
from jax import lax
from jax.experimental import pallas as pl
from jax.experimental.pallas import tpu as pltpu
from jax.sharding import PartitionSpec as P

HEAD_SIZE = 128
QSCALE = 168
WINDOW = 1024
NH, NZ, NY, NHEAD = 2, 16, 4, 4
SEQ = NH * NZ * NY
TOK = 128
WIDTH = 2688
ROWS = WIDTH // SEQ
SLOT = 64
FSLOT = 48
GROUP = 16
SPAN = GROUP * ROWS
WIN = 512
EDGE = 384
F32 = jnp.float32
BF16 = jnp.bfloat16


def dot(a, b, ca=1, cb=0):
    return lax.dot_general(a, b, (((ca,), (cb,)), ((), ())), preferred_element_type=F32)


def iota(shape, axis):
    return lax.broadcasted_iota(jnp.int32, shape, axis)


def rotary(normed, cosine, sine):
    return normed * cosine + pltpu.roll(normed, HEAD_SIZE // 2, 1) * sine


def norm_forward(raw, gain, cosine, sine):
    inv = lax.rsqrt(jnp.mean(raw * raw, axis=1, keepdims=True) + 1e-06)
    return rotary(raw * inv * gain, cosine, sine)


def norm_backward(grad, raw, gain, cosine, sine):
    inv = lax.rsqrt(jnp.mean(raw * raw, axis=1, keepdims=True) + 1e-06)
    back = (grad * cosine + pltpu.roll(grad * sine, HEAD_SIZE // 2, 1)) * gain
    along = jnp.mean(raw * back, axis=1, keepdims=True)
    return inv * (back - raw * (inv * inv * along))


def body(
    x_hbm, g_hbm, wk_ref, wv_ref, wq_ref, wo_ref, start_ref, cos_ref, sin_ref, qg_ref, kg_ref,
    gi_ref, fv_ref,
    x_ref, g_ref, squares, full, lhs, acc, ctx, dctx, ret, tree, treeback, qn, dqn, total, parts, arrived,
    fpad, ftwo, fsend, fy, flow, fmid, flo, flsend, usend, urecv, last, zsend, zrecv,
    kvraw,
    send_sem, recv_sem, local_sem,
):
    s = lax.axis_index("seq")
    hd = lax.axis_index("head")
    h = s // (NZ * NY)
    z = lax.rem(s // NY, NZ)
    y = lax.rem(s, NY)
    base = h * (NZ * NY)

    def at_z(step):
        return base + lax.rem(z + step + NZ, NZ) * NY + y

    def at_y(step):
        return base + z * NY + lax.rem(y + step + NY, NY)

    def shifted(step):
        return lax.rem(s + step + SEQ, SEQ)

    zi = lambda step: lax.rem(z + step + 2 * NZ, NZ)
    yi = lambda step: lax.rem(y + step + NY, NY)
    across = (1 - h) * (NZ * NY) + z * NY + y

    barrier = pltpu.get_barrier_semaphore()
    seq_partners = [at_z(1), at_z(-1), at_y(1), at_y(2), at_y(3), across]
    seq_partners += [shifted(4), shifted(-4), shifted(8), shifted(-8)]
    for partner in seq_partners:
        pl.semaphore_signal(barrier, inc=1, device_id={"seq": partner})
    for e in range(1, NHEAD):
        pl.semaphore_signal(barrier, inc=1, device_id={"head": lax.rem(hd + e, NHEAD)})
    load_x = pltpu.make_async_copy(x_hbm, x_ref, local_sem.at[0])
    load_g = pltpu.make_async_copy(g_hbm, g_ref, local_sem.at[1])
    load_x.start()
    load_g.start()

    def rows_at(first):
        return jnp.where(
            iota((SLOT, ROWS), 0) == iota((SLOT, ROWS), 1) + first, 1.0, 0.0
        ).astype(BF16)

    rest = dot(rows_at(ROWS), wq_ref[...]) + dot(rows_at(2 * ROWS), wo_ref[...])
    own_slot = full.at[h, z, y]
    own_slot[:, 0:256] = (dot(rows_at(0), wk_ref[...]) + rest[:, 0:256]).astype(BF16)
    own_slot[:, 256:512] = (dot(rows_at(0), wv_ref[...]) + rest[:, 256:512]).astype(BF16)
    pl.semaphore_wait(barrier, len(seq_partners) + NHEAD - 1)

    def remote(src, dst, sem, target, axis="seq"):
        return pltpu.make_async_remote_copy(
            src_ref=src,
            dst_ref=dst,
            send_sem=send_sem.at[sem],
            recv_sem=recv_sem.at[sem],
            device_id={axis: target},
        )

    def here(dst, sem):
        return remote(dst, dst, sem, across)

    HX = 0
    AZ = HX + 1
    BZ = AZ + 32
    AY = BZ + 32
    BY = AY + 96
    BX = BY + 4
    KV = BX + 16
    DK = KV + 8
    GR = DK + 16
    FY = GR + 3
    FL = FY + 6
    FH = FL + 6
    FZ = FH + 2
    HY = FZ + 15
    CY = HY + 1
    CZ = CY + 4
    KX = CZ + 16

    side_z = lambda side: at_z(1 if side == 0 else -1)
    xs = (h, 1 - h)

    def a_piece(c, zz, yy):
        return full.at[xs[c], zz, yy, pl.ds(0, 32), :]

    def b_piece(zz, b):
        return full.at[h, zz, :, pl.ds(32 + 16 * b, 16), :]

    def az(c, k, side):
        ref = a_piece(c, zi(1 - k) if side == 0 else zi(k - 1), y)
        return remote(ref, ref, AZ + 16 * c + 2 * (k - 1) + side, side_z(side))

    def az_in(c, k, side):
        ref = a_piece(c, zi(-k) if side == 0 else zi(k), y)
        return here(ref, AZ + 16 * c + 2 * (k - 1) + side)

    def bz(b, k, side):
        ref = b_piece(zi(1 - k) if side == 0 else zi(k - 1), b)
        return remote(ref, ref, BZ + 16 * b + 2 * (k - 1) + side, side_z(side))

    def bz_in(b, k, side):
        ref = b_piece(zi(-k) if side == 0 else zi(k), b)
        return here(ref, BZ + 16 * b + 2 * (k - 1) + side)

    def bx(step, index):
        ref = full.at[h, zi(step), :, pl.ds(32, 32), pl.ds(0, EDGE)]
        return remote(ref, ref, BX + index, across)

    def bx_in(step, index):
        return here(full.at[1 - h, zi(step), :, pl.ds(32, 32), pl.ds(0, EDGE)], BX + index)

    def c_piece(zz):
        return full.at[1 - h, zz, :, pl.ds(32, 32), pl.ds(EDGE, 512 - EDGE)]

    def cz(k, side):
        ref = c_piece(zi(1 - k) if side == 0 else zi(k - 1))
        return remote(ref, ref, CZ + 2 * (k - 1) + side, side_z(side))

    def cz_in(k, side):
        return here(c_piece(zi(-k) if side == 0 else zi(k)), CZ + 2 * (k - 1) + side)

    left, right, far = yi(3), yi(1), yi(2)

    def ay_start(c, step, index):
        sem = AY + 48 * c + 3 * index
        own = a_piece(c, zi(step), y)
        remote(own, own, sem, at_y(1)).start()
        remote(own, own, sem + 1, at_y(3)).start()

    def ay_forward(c, step, index):
        sem = AY + 48 * c + 3 * index
        zz = zi(step)
        here(a_piece(c, zz, left), sem).wait_recv()
        here(a_piece(c, zz, right), sem + 1).wait_recv()
        ref = a_piece(c, zz, right if c else left)
        remote(ref, ref, sem + 2, at_y(3 if c else 1)).start()

    def ay_finish(c, step, index):
        sem = AY + 48 * c + 3 * index
        zz = zi(step)
        here(a_piece(c, zz, far), sem + 2).wait_recv()
        own = a_piece(c, zz, y)
        for i in range(3):
            here(own, sem + i).wait_send()

    def place_of(k, side):
        return (-k if side == 0 else k), 2 * k - 1 + side

    def first_step(k, final=False):
        for c in range(2):
            for side in range(2):
                az_in(c, k, side).wait_recv()
                if not final or side == c:
                    az(c, k + 1, side).start()
                ay_start(c, *place_of(k, side))

    def hx_piece(hh, lo, first):
        return full.at[hh, z, y, pl.ds(lo, 32), pl.ds(first, 512 - first)]

    cross = [
        remote(hx_piece(h, lo, first), hx_piece(h, lo, first), sem, across)
        for lo, first, sem in ((0, 0, HX), (32, EDGE, HY))
    ]
    for copy in cross:
        copy.start()

    def by_piece(yy, lo, n):
        return full.at[h, z, yy, pl.ds(lo, n), :]

    mine = by_piece(y, 32, 32)
    by_first = [remote(mine, mine, BY, at_y(1)), remote(mine, mine, BY + 1, at_y(3))]
    for copy in by_first:
        copy.start()
    for side in range(2):
        az(0, 1, side).start()
    ay_start(0, 0, 0)
    here(a_piece(1, z, y), HX).wait_recv()
    for side in range(2):
        az(1, 1, side).start()
    ay_start(1, 0, 0)
    here(hx_piece(1 - h, 32, EDGE), HY).wait_recv()

    def cy_piece(yy, lo, n):
        return full.at[1 - h, z, yy, pl.ds(lo, n), pl.ds(EDGE, 512 - EDGE)]

    mine = cy_piece(y, 32, 32)
    cy_first = [remote(mine, mine, CY, at_y(1)), remote(mine, mine, CY + 1, at_y(3))]
    for copy in cy_first:
        copy.start()
    up, down = by_piece(left, 32, 16), by_piece(right, 48, 16)
    by_second = [remote(up, up, BY + 2, at_y(1)), remote(down, down, BY + 3, at_y(3))]
    here(by_piece(left, 32, 32), BY).wait_recv()
    by_second[0].start()
    here(by_piece(right, 32, 32), BY + 1).wait_recv()
    by_second[1].start()
    first_step(1)
    for i in range(2):
        here(by_piece(far, 32 + 16 * i, 16), BY + 2 + i).wait_recv()
        for side in range(2):
            bz(i, 1, side).start()
    bx(0, 0).start()
    up, down = cy_piece(left, 32, 16), cy_piece(right, 48, 16)
    cy_second = [remote(up, up, CY + 2, at_y(1)), remote(down, down, CY + 3, at_y(3))]
    here(cy_piece(left, 32, 32), CY).wait_recv()
    cy_second[0].start()
    here(cy_piece(right, 32, 32), CY + 1).wait_recv()
    cy_second[1].start()
    first_step(2)
    for i in range(2):
        here(cy_piece(far, 32 + 16 * i, 16), CY + 2 + i).wait_recv()
    for side in range(2):
        cz(1, side).start()

    def selection(j):
        first_row = SPAN * j
        low = jnp.minimum((first_row // 128) * 128, WIDTH - WIN)
        return pl.multiple_of(low, 128), first_row - low

    def prepare(j):
        low, offset = selection(j)
        column = iota((1, GROUP * SLOT), 1)
        slot = column & (SLOT - 1)
        target = jnp.where(slot < ROWS, offset + (column >> 6) * ROWS + slot, -1)
        select = jnp.where(iota((WIN, GROUP * SLOT), 0) == target, 1.0, 0.0).astype(BF16)
        spread = dot(x_ref[:, pl.ds(low, WIN)], select)
        lhs[j, 0:TOK] = spread.astype(BF16)
        lhs[j, TOK : 2 * TOK] = pltpu.roll(spread, ROWS, 1).astype(BF16)
        spread = dot(g_ref[:, pl.ds(low, WIN)], select)
        lhs[j, 2 * TOK :] = pltpu.roll(spread, 2 * ROWS, 1).astype(BF16)
        row = iota((GROUP * FSLOT, 1), 0)
        owner = (row * 1366) >> 16
        slot = row - owner * FSLOT
        slot = jnp.where(slot < ROWS, slot, slot - ROWS)
        target = jnp.where(slot < ROWS, offset + owner * ROWS + slot, -1)
        select = jnp.where(iota((GROUP * FSLOT, WIN), 1) == target, 1.0, 0.0).astype(BF16)
        block = x_ref[:, pl.ds(low, WIN)].astype(F32)
        squares[j] = dot(select, (block * block).astype(BF16), 1, 1).astype(BF16)

    def step_of(k, final=False):
        for b in range(2):
            for side in range(2):
                bz_in(b, k, side).wait_recv()
                if not final or side == b:
                    bz(b, k + 1, side).start()
        for side in range(2):
            bx(*place_of(k, side)).start()
        for side in range(2):
            cz_in(k, side).wait_recv()
            if not final or side == 0:
                cz(k + 1, side).start()

    def forward_of(k):
        for c in range(2):
            for side in range(2):
                ay_forward(c, *place_of(k, side))

    load_x.wait()
    load_g.wait()
    prepare(0)
    step_of(1)
    first_step(3)
    for c in range(2):
        ay_forward(c, 0, 0)
    forward_of(1)

    def steps(k, carry):
        step_of(k)
        first_step(k + 2)
        forward_of(k)
        prepare(k - 1)
        return carry

    lax.fori_loop(2, 5, steps, 0)
    step_of(5)
    first_step(7, True)
    forward_of(5)
    prepare(4)
    step_of(6)
    for c in range(2):
        az_in(c, 8, c).wait_recv()
        ay_start(c, 8, 15)
    forward_of(6)
    prepare(5)
    step_of(7, True)
    forward_of(7)
    prepare(6)
    for c in range(2):
        ay_forward(c, 8, 15)
    for b in range(2):
        bz_in(b, 8, b).wait_recv()
    bx(8, 15).start()
    cz_in(8, 0).wait_recv()
    prepare(7)

    for copy in cross + by_first + by_second + cy_first + cy_second:
        copy.wait_send()
    for c in range(2):
        ay_finish(c, 0, 0)
    bx_in(0, 0).wait_recv()
    bx(0, 0).wait_send()

    def finish(k, carry):
        for side in range(2):
            for c in range(2):
                az(c, k, side).wait_send()
                bz(c, k, side).wait_send()
                ay_finish(c, *place_of(k, side))
            bx_in(*place_of(k, side)).wait_recv()
            bx(*place_of(k, side)).wait_send()
            cz(k, side).wait_send()
        return carry

    lax.fori_loop(1, 8, finish, 0)
    for c in range(2):
        az(c, 8, c).wait_send()
        bz(c, 8, c).wait_send()
        ay_finish(c, 8, 15)
    bx_in(8, 15).wait_recv()
    bx(8, 15).wait_send()
    cz(8, 0).wait_send()

    def weights(j):
        return full[j // 4, pl.ds(4 * lax.rem(j, 4), 4)].reshape(GROUP * SLOT, 512)

    acc[...] = jnp.zeros_like(acc)

    def project(lo, hi):
        def run(j, carry):
            acc[lo:hi] += dot(lhs[j, lo:hi], weights(j))
            return carry

        lax.fori_loop(0, SEQ // GROUP, run, 0)

    project(0, TOK)
    cosine = jnp.concatenate([cos_ref[...], cos_ref[...]], axis=1)
    sine = jnp.concatenate([-sin_ref[...], sin_ref[...]], axis=1)
    q_gain, k_gain = qg_ref[...], kg_ref[...]
    for i in range(2):
        cols = slice(i * 128, (i + 1) * 128)
        ctx[0, 0, :, cols] = norm_forward(acc[0:TOK, cols], k_gain, cosine, sine).astype(BF16)
    ctx[0, 1] = acc[0:TOK, 256:512].astype(BF16)

    hop4 = [remote(ctx.at[0, i], ctx.at[4, i], (KV, KX)[i], shifted(4)) for i in range(2)]
    hop8 = [remote(ctx.at[4, i], ctx.at[8, i], (KV, KX)[i] + 1, shifted(4)) for i in range(2)]
    for copy in hop4:
        copy.start()

    def side_copies(e):
        low = jnp.where(y + e < NY, 0, 4)
        one = remote(ctx.at[low], ctx.at[e], KV + 2 * e, at_y(e))
        two = remote(ctx.at[low + 4], ctx.at[e + 4], KV + 2 * e + 1, at_y(e))
        return one, two

    for e in range(1, NY):
        @pl.when(y + e < NY)
        def _():
            side_copies(e)[0].start()
    for i in range(2):
        here(ctx.at[4, i], (KV, KX)[i]).wait_recv()
        hop8[i].start()
    for e in range(1, NY):
        @pl.when(y + e < NY)
        def _():
            side_copies(e)[1].start()

        @pl.when(y + e >= NY)
        def _():
            side_copies(e)[0].start()
    project(TOK, 3 * TOK)
    for i in range(2):
        here(ctx.at[8, i], (KV, KX)[i] + 1).wait_recv()
    for e in range(1, NY):
        @pl.when(y + e >= NY)
        def _():
            side_copies(e)[1].start()
    for i in range(4):
        cols = slice(i * 128, (i + 1) * 128)
        half = slice((i % 2) * TOK, (i % 2 + 1) * TOK)
        qn[i // 2, half] = norm_forward(
            acc[TOK : 2 * TOK, cols], q_gain, cosine, sine
        ).astype(BF16)
        dqn[i // 2, half] = acc[2 * TOK :, cols].astype(BF16)
    for e in range(1, NY):
        here(ctx.at[e], KV + 2 * e).wait_recv()
        here(ctx.at[e + 4], KV + 2 * e + 1).wait_recv()
    for copy in hop4 + hop8:
        copy.wait_send()
    for e in range(1, NY):
        one, two = side_copies(e)
        one.wait_send()
        two.wait_send()

    scale = float(QSCALE) ** (-0.5)
    reach = 9 * TOK
    place = iota((reach, 1), 0)
    key_index = s * TOK - (place & ~(TOK - 1)) + (place & (TOK - 1))
    query_index = s * TOK + (iota((1, 2 * TOK), 1) & (TOK - 1))
    visible = (
        (key_index >= jnp.concatenate([start_ref[...], start_ref[...]], axis=1))
        & (key_index <= query_index)
        & (query_index - key_index < WINDOW)
    )
    for i in range(2):
        cols = slice(i * 128, (i + 1) * 128)
        keys = ctx[:, 0, :, cols].reshape(reach, 128)
        values = ctx[:, 1, :, cols].reshape(reach, 128)
        queries, douts = qn[i], dqn[i]
        scores = jnp.where(visible, dot(keys, queries, 1, 1) * scale, -jnp.inf)
        expd = jnp.exp(scores - jnp.max(scores, axis=0, keepdims=True))
        probs = expd * (1.0 / jnp.sum(expd, axis=0, keepdims=True))
        dprobs = dot(values, douts, 1, 1)
        delta = jnp.sum(probs * dprobs, axis=0, keepdims=True)
        dscores = (probs * (dprobs - delta)).astype(BF16)
        dctx[:, 0, :, cols] = (dot(dscores, queries) * scale).astype(BF16).reshape(9, TOK, 128)
        dctx[:, 1, :, cols] = dot(probs.astype(BF16), douts).astype(BF16).reshape(9, TOK, 128)
        dquery = dot(dscores, keys, 0, 0) * scale
        for r in range(2):
            col = slice((2 * i + r) * 128, (2 * i + r + 1) * 128)
            kvraw[0, :, col] = norm_backward(
                dquery[r * TOK : (r + 1) * TOK], acc[TOK : 2 * TOK, col], q_gain, cosine, sine
            ).astype(BF16)

    def side_back(e, which):
        sem = DK + 6 * which + 2 * (e - 1)
        return [
            remote(dctx.at[e + 4 * i, which], ret.at[e - 1, i, which], sem + i, at_y(NY - e))
            for i in range(2)
        ]

    def tree_back(which):
        sem = DK + 12 + 2 * which
        return [
            remote(tree.at[which, i], treeback.at[which, i], sem + i, shifted(-4 * (i + 1)))
            for i in range(2)
        ]

    for which in (1, 0):
        for e in range(1, NY):
            for copy in side_back(e, which):
                copy.start()

    def gather_sums(which):
        sums = [dctx[4 * i, which].astype(F32) for i in range(3)]
        for e in range(1, NY):
            for i in range(2):
                here(ret.at[e - 1, i, which], DK + 6 * which + 2 * (e - 1) + i).wait_recv()
            same = y + e < NY
            one = ret[e - 1, 0, which].astype(F32)
            two = ret[e - 1, 1, which].astype(F32)
            sums[0] += jnp.where(same, one, 0.0)
            sums[1] += jnp.where(same, two, one)
            sums[2] += jnp.where(same, 0.0, two)
        tree[which, 0] = sums[1].astype(BF16)
        tree[which, 1] = sums[2].astype(BF16)
        for copy in tree_back(which):
            copy.start()
        return sums[0]

    def whole(which, own):
        for i in range(2):
            here(treeback.at[which, i], DK + 12 + 2 * which + i).wait_recv()
            own = own + treeback[which, i].astype(F32)
        return own

    total[...] = jnp.zeros_like(total)

    def spread_back(which, lo, hi):
        low_slot = ROWS if which == 0 else 0

        def run(j, carry):
            low, offset = selection(j)
            out = dot(kvraw[which], weights(j), 1, 1).astype(BF16)
            row = iota((GROUP * SLOT, 1), 0)
            slot = (row & (SLOT - 1)) - low_slot
            target = jnp.where(
                (slot >= 0) & (slot < ROWS), offset + (row >> 6) * ROWS + slot, -1
            )
            select = jnp.where(iota((GROUP * SLOT, WIN), 1) == target, 1.0, 0.0).astype(BF16)
            total[:, pl.ds(low, WIN)] += dot(out, select)
            return carry

        lax.fori_loop(lo, hi, run, 0)

    spread_back(0, 0, 4)
    own_dv = gather_sums(1)
    own_dk = gather_sums(0)
    dvalue = whole(1, own_dv)

    first_cols = jnp.where(iota((GROUP, FSLOT, 128), 1) < ROWS, 1.0, 0.0)
    dv_sq = (dvalue * dvalue).astype(BF16)

    def slots(half, low):
        j = 4 * half + low
        both = dot(squares[j], dv_sq)
        both = both.reshape(GROUP, FSLOT, 256)
        picked = jnp.where(first_cols > 0.5, both[:, :, 0:128], both[:, :, 128:256])
        fpad[half, 4 * low : 4 * low + 4] = picked.astype(BF16).reshape(4, 4, FSLOT, 128)

    for low in range(2):
        slots(1 - h, low)

    cross_low = remote(fpad.at[1 - h, pl.ds(0, 8)], flow, FH, across)
    cross_low.start()

    def ring(pick, buf, sem):
        return [
            remote(pick(0, far), buf.at[0], sem, at_y(1)),
            remote(pick(1, far), buf.at[1], sem + 1, at_y(3)),
            remote(pick(1, right), buf.at[2], sem + 2, at_y(1)),
            remote(pick(0, left), buf.at[3], sem + 3, at_y(3)),
        ]

    def ring_next(pick_value, buf, send, sem):
        here(buf.at[0], sem).wait_recv()
        send[0] = (pick_value(0, right) + buf[0].astype(F32)).astype(BF16)
        one = remote(send.at[0], buf.at[4], sem + 4, at_y(1))
        one.start()
        here(buf.at[1], sem + 1).wait_recv()
        send[1] = (pick_value(1, left) + buf[1].astype(F32)).astype(BF16)
        two = remote(send.at[1], buf.at[5], sem + 5, at_y(3))
        two.start()
        return [one, two]

    def ring_end(pick_value, buf, sem):
        for i in range(2, 6):
            here(buf.at[i], sem + i).wait_recv()
        first = pick_value(0, y) + buf[4].astype(F32) + buf[3].astype(F32)
        second = pick_value(1, y) + buf[2].astype(F32) + buf[5].astype(F32)
        return first, second

    up_ring = ring(lambda i, yy: fpad.at[i, pl.ds(8, 8), yy], ftwo, FY)
    for half in range(2):
        for low in range(2, 4):
            slots(half, low)
    for copy in up_ring:
        copy.start()
    for low in range(2):
        slots(h, low)
    spread_back(0, 4, 8)
    up_value = lambda i, yy: fpad[i, 8:16, yy].astype(F32)
    up_ring += ring_next(up_value, ftwo, fsend, FY)

    here(flow, FH).wait_recv()
    fmid[...] = (fpad[h, 0:8].astype(F32) + flow[...].astype(F32)).astype(BF16)
    low_ring = ring(lambda i, yy: fmid.at[pl.ds(4 * i, 4), yy], flo, FL)
    for copy in low_ring:
        copy.start()

    dkey = whole(0, own_dk)
    for i in range(2):
        cols = slice(i * 128, (i + 1) * 128)
        kvraw[1, :, cols] = norm_backward(
            dkey[:, cols], acc[0:TOK, cols], k_gain, cosine, sine
        ).astype(BF16)
    kvraw[1, :, 256:512] = dvalue.astype(BF16)
    spread_back(1, 0, 2)

    fy[0], fy[1] = ring_end(up_value, ftwo, FY)
    usend[...] = fy[1 - h].astype(BF16)
    cross_up = remote(usend, urecv, FH + 1, across)
    cross_up.start()
    low_value = lambda i, yy: fmid[4 * i : 4 * i + 4, yy].astype(F32)
    low_ring += ring_next(low_value, flo, flsend, FL)

    spread_back(1, 2, 5)
    last[0:4], last[4:8] = ring_end(low_value, flo, FL)
    here(urecv, FH + 1).wait_recv()
    last[8:16] = fy[h] + urecv[...].astype(F32)
    zsend[...] = last[...].astype(BF16)

    def to_z(d):
        return remote(zsend.at[zi(d)], zrecv.at[d - 1], FZ + d - 1, at_z(d))

    for d in (8, 7, 9, 6, 10, 5, 11, 4, 12, 3, 13, 2, 14, 1, 15):
        to_z(d).start()

    spread_back(1, 5, 8)
    for i in range(NHEAD):
        parts[i] = total[i * 32 : (i + 1) * 32].astype(BF16)
    shares = []
    for e in range(1, NHEAD):
        to = lax.rem(hd + e, NHEAD)
        shares.append(remote(parts.at[to], arrived.at[e - 1], GR + e - 1, to, "head"))
        shares[-1].start()

    sums = last[z]
    for d in range(1, NZ):
        here(zrecv.at[d - 1], FZ + d - 1).wait_recv()
        sums = sums + zrecv[d - 1].astype(F32)
    sums = sums * (1.0 / (SEQ * TOK))
    fv_ref[:, 0:128] = sums[0:ROWS]
    fv_ref[:, 128:256] = pltpu.roll(sums, FSLOT - ROWS, 0)[0:ROWS]

    for e in range(1, NHEAD):
        here(arrived.at[e - 1], GR + e - 1).wait_recv()
    mine = total[pl.ds(pl.multiple_of(hd * 32, 32), 32)]
    for e in range(1, NHEAD):
        mine = mine + arrived[e - 1].astype(F32)
    gi_ref[...] = mine.astype(BF16)

    for copy in shares + up_ring + low_ring + [cross_low, cross_up]:
        copy.wait_send()
    for d in range(1, NZ):
        to_z(d).wait_send()
    for which in range(2):
        for copy in tree_back(which):
            copy.wait_send()
        for e in range(1, NY):
            for copy in side_back(e, which):
                copy.wait_send()


def layer(*operands):
    vmem = pl.BlockSpec(memory_space=pltpu.VMEM)
    sems = 320
    return pl.pallas_call(
        body,
        name="layer_backward",
        out_shape=(
            jax.ShapeDtypeStruct((32, WIDTH), BF16),
            jax.ShapeDtypeStruct((ROWS, 256), F32),
        ),
        in_specs=[pl.BlockSpec(memory_space=pl.ANY)] * 2 + [vmem] * 9,
        out_specs=(vmem, vmem),
        scratch_shapes=[
            pltpu.VMEM((TOK, WIDTH), BF16),
            pltpu.VMEM((TOK, WIDTH), BF16),
            pltpu.VMEM((SEQ // GROUP, GROUP * FSLOT, TOK), BF16),
            pltpu.VMEM((NH, NZ, NY, SLOT, 512), BF16),
            pltpu.VMEM((SEQ // GROUP, 3 * TOK, GROUP * SLOT), BF16),
            pltpu.VMEM((3 * TOK, 512), F32),
            pltpu.VMEM((9, 2, TOK, 256), BF16),
            pltpu.VMEM((9, 2, TOK, 256), BF16),
            pltpu.VMEM((3, 2, 2, TOK, 256), BF16),
            pltpu.VMEM((2, 2, TOK, 256), BF16),
            pltpu.VMEM((2, 2, TOK, 256), BF16),
            pltpu.VMEM((2, 2 * TOK, 128), BF16),
            pltpu.VMEM((2, 2 * TOK, 128), BF16),
            pltpu.VMEM((TOK, WIDTH), F32),
            pltpu.VMEM((NHEAD, 32, WIDTH), BF16),
            pltpu.VMEM((NHEAD - 1, 32, WIDTH), BF16),
            pltpu.VMEM((NH, NZ, NY, FSLOT, 128), BF16),
            pltpu.VMEM((6, 8, FSLOT, 128), BF16),
            pltpu.VMEM((2, 8, FSLOT, 128), BF16),
            pltpu.VMEM((NH, 8, FSLOT, 128), F32),
            pltpu.VMEM((8, NY, FSLOT, 128), BF16),
            pltpu.VMEM((8, NY, FSLOT, 128), BF16),
            pltpu.VMEM((6, 4, FSLOT, 128), BF16),
            pltpu.VMEM((2, 4, FSLOT, 128), BF16),
            pltpu.VMEM((8, FSLOT, 128), BF16),
            pltpu.VMEM((8, FSLOT, 128), BF16),
            pltpu.VMEM((NZ, FSLOT, 128), F32),
            pltpu.VMEM((NZ, FSLOT, 128), BF16),
            pltpu.VMEM((NZ - 1, FSLOT, 128), BF16),
            pltpu.VMEM((2, TOK, 512), BF16),
            pltpu.SemaphoreType.DMA((sems,)),
            pltpu.SemaphoreType.DMA((sems,)),
            pltpu.SemaphoreType.DMA((2,)),
        ],
        compiler_params=pltpu.CompilerParams(
            collective_id=0, has_side_effects=True, vmem_limit_bytes=60 * 1024 * 1024
        ),
    )(*operands)


def on_device(
    layer_input,
    grad_out,
    doc_start,
    w_query,
    key_weight,
    value_weight,
    w_out,
    q_gain,
    key_norm_gain,
):
    seq_index = lax.axis_index("seq")
    token_index = seq_index * TOK + jnp.arange(TOK, dtype=jnp.int32)
    positions = (token_index - doc_start).astype(F32)
    half = HEAD_SIZE // 2
    frequency = jnp.exp(jnp.arange(half).astype(F32) * (-math.log(10000.0) / half))
    angles = positions[:, None] * frequency[None, :]
    cosine, sine = jnp.cos(angles), jnp.sin(angles)
    grad_input, fisher_value = layer(
        layer_input, grad_out, key_weight, value_weight, w_query, w_out.T, doc_start[None, :],
        cosine, sine,
        q_gain[None, :], key_norm_gain[None, :],
    )
    return (fisher_value, grad_input)


def solution(mesh):
    in_specs = (
        P("seq", None),
        P("seq", None),
        P("seq"),
        P("seq", "head"),
        P("seq", "head"),
        P("seq", "head"),
        P("head", "seq"),
        P(),
        P(),
    )
    out_specs = (P("seq", "head"), P(("seq", "head"), None))
    return jax.shard_map(
        on_device, mesh=mesh, in_specs=in_specs, out_specs=out_specs, check_vma=False
    )
```
